32 devices in a mesh: lat: 4 (over y, x), lon: 8 (over z, core).
Axes of the slice: x: 2, y: 2, z: 4, core: 2. Of those that a mesh axis runs over, the one named last changes fastest.
Arguments:
- analysis_vector: float32 [69, 64, 1024], P(None, 'lat', 'lon'), may hold values from -6 to 6
- prior_estimate: float32 [69, 64, 1024], P(None, 'lat', 'lon'), may hold values from -6 to 6
- prior_precision: float32 [69], replicated, may hold values from 0.5 to 2
- encoder_weight: bfloat16 [69, 256], replicated, may hold values from -0.75 to 0.75
- conv_weights: bfloat16 [2, 3, 3, 256, 256], replicated, may hold values from -0.125 to 0.125
- readout_matrix: bfloat16 [256, 69], replicated, may hold values from -0.375 to 0.375
- obs_in_weight: bfloat16 [4, 69, 1024], replicated, may hold values from -0.375 to 0.375
- obs_out_weight: bfloat16 [1024, 128], replicated, may hold values from -0.1875 to 0.1875
- obs_values: float32 [65536, 128], P(('lat', 'lon')), may hold values from -6 to 6
- obs_precision: float32 [128], replicated, may hold values from 0.5 to 2
- foot_cells: int32 [65536, 4], P(('lat', 'lon')), may hold values from 0 to 65535, as said below
- obs_count: int32 [32], P(('lat', 'lon')), may hold values from 512 to 2048, as said below
Outputs:
- departures: float32 [65536, 128], P(('lat', 'lon'))
- cost_derivative: float32 [69, 64, 1024], P(None, 'lat', 'lon')
The draws below stay inside these ranges and needn't reach their ends.
Inputs may be any that keep to these rules, and one draw needn't show every extreme that they name: `foot_cells`: each observation's 4 columns form a 2x2 block of neighbouring cells inside one device's tile. Each device has its own order of all 32 tiles, drawn from the seed, and its observation slot o (counted within the device) lies on the tile at place o mod 32 of that order, so that every device puts exactly 256 footprint columns of its slots on every tile. `obs_count`: the devices of at least one latitude row of the mesh (a swath), sometimes more rows, have 2048 valid observations; every other device has between 512 and 682.
All inputs are finite; a program needn't handle non-finite values.
Results may differ from the reference program's by a relative error of at most 0.008.
Values may be sent and summed in bfloat16 or wider, within the bound.
No kernel may reach another device: no remote copies, remote signals or barrier semaphores. Data moves between devices by JAX's collectives and lax.ppermute only.
A program may use at most 128 MiB of HBM per device.

```python
import math
import jax
import jax.numpy as jnp
from jax import lax

PROGNOSTIC_VARS = 69
CH = 256
LAYERS = 2
OBS_HID = 1024
NCH = 128
FOOT = 4
CLAT = 16
CLON = 128
OBS_DEV = 2048
TILES = 32
MERIDIAN_POINTS = 64
ZONAL_POINTS = 1024
OBS_TOTAL = 65536


def draw_obs_count(key, part):
    lat_rows = MERIDIAN_POINTS // CLAT
    lon_rows = ZONAL_POINTS // CLON
    tile_count = lat_rows * lon_rows
    key_low, key_row, key_extra = jax.random.split(key, 3)
    low_counts = jax.random.randint(key_low, (tile_count,), OBS_DEV // 4, OBS_DEV // 3 + 1)
    swath_row = jax.random.randint(key_row, (), 0, lat_rows)
    extra_rows = jax.random.randint(key_extra, (lat_rows,), 0, 4) == 0
    tile_lat = jnp.arange(tile_count) // lon_rows
    full_tile = jnp.logical_or(tile_lat == swath_row, extra_rows[tile_lat])
    return jnp.where(full_tile, OBS_DEV, low_counts).astype(jnp.int32)


def draw_foot_cells(key, part):
    lat_rows = MERIDIAN_POINTS // CLAT
    lon_rows = ZONAL_POINTS // CLON
    tile_count = lat_rows * lon_rows
    key_perm, key_row, key_col = jax.random.split(key, 3)
    orders = jax.vmap(lambda one_key: jax.random.permutation(one_key, tile_count))(jax.random.split(key_perm, tile_count))
    holder = orders[:, jnp.arange(OBS_DEV) % tile_count]
    row_in = jax.random.randint(key_row, (tile_count, OBS_DEV), 0, CLAT - 1)
    col_in = jax.random.randint(key_col, (tile_count, OBS_DEV), 0, CLON - 1)
    base_row = holder // lon_rows * CLAT + row_in
    base_col = holder % lon_rows * CLON + col_in
    step_row = jnp.array([0, 1, 0, 1], jnp.int32)
    step_col = jnp.array([0, 0, 1, 1], jnp.int32)
    cell_ids = (base_row[:, :, None] + step_row) * ZONAL_POINTS + base_col[:, :, None] + step_col
    return cell_ids.reshape(tile_count * OBS_DEV, FOOT).astype(jnp.int32)


def block_scale(key, shape, cuts, least, high):
    factor_of, own = 1.0, jax.random.fold_in(key, 6)
    for axis_at, shards_of in cuts:
        steps = jnp.exp(jax.random.uniform(jax.random.fold_in(own, axis_at), (shards_of,), jnp.float32, least / len(cuts), high / len(cuts)))
        factor_of = factor_of * jnp.repeat(steps, shape[axis_at] // shards_of).reshape([-1 if axis == axis_at else 1 for axis in range(len(shape))])
    return factor_of


def gaussian(key, extent, deviation, bound, cuts=(), kind=jnp.bfloat16):
    drawn = jax.random.normal(key, extent, jnp.float32) * deviation
    if len(cuts) > 0:
        drawn = block_scale(key, extent, cuts, -0.22, 0.18) * drawn
    return jnp.clip(drawn, min=-bound, max=bound).astype(kind)


def setup_inputs(seed: int = 0) -> dict:
    arg_keys = jax.random.split(jax.random.key(seed), 13)
    return {
        "analysis_vector": gaussian(arg_keys[0], (PROGNOSTIC_VARS, MERIDIAN_POINTS, ZONAL_POINTS), 1.0, 6.0, ((1, 4), (2, 8)), jnp.float32),
        "prior_estimate": gaussian(arg_keys[1], (PROGNOSTIC_VARS, MERIDIAN_POINTS, ZONAL_POINTS), 1.0, 6.0, ((1, 4), (2, 8)), jnp.float32),
        "prior_precision": jnp.clip(jnp.exp(jax.random.uniform(arg_keys[2], (PROGNOSTIC_VARS,), jnp.float32, math.log(0.5), math.log(2.0))), 0.5, 2.0),
        "encoder_weight": gaussian(arg_keys[3], (PROGNOSTIC_VARS, CH), PROGNOSTIC_VARS ** -0.5, 0.75),
        "conv_weights": gaussian(arg_keys[4], (LAYERS, 3, 3, CH, CH), (9 * CH) ** -0.5, 0.125),
        "readout_matrix": gaussian(arg_keys[5], (CH, PROGNOSTIC_VARS), CH ** -0.5, 0.375),
        "obs_in_weight": gaussian(arg_keys[6], (FOOT, PROGNOSTIC_VARS, OBS_HID), (FOOT * PROGNOSTIC_VARS) ** -0.5, 0.375),
        "obs_out_weight": gaussian(arg_keys[7], (OBS_HID, NCH), OBS_HID ** -0.5, 0.1875),
        "obs_values": gaussian(arg_keys[8], (OBS_TOTAL, NCH), 1.0, 6.0, ((0, 32),), jnp.float32),
        "obs_precision": jnp.clip(jnp.exp(jax.random.uniform(arg_keys[9], (NCH,), jnp.float32, math.log(0.5), math.log(2.0))), 0.5, 2.0),
        "foot_cells": draw_foot_cells(jax.random.fold_in(arg_keys[12], 71), 0),
        "obs_count": draw_obs_count(jax.random.fold_in(arg_keys[12], 71), 0),
    }


def silu_slope(values):
    sigma_val = jax.nn.sigmoid(values)
    return sigma_val * (1.0 + values * (1.0 - sigma_val))


def wrap_conv(field_in, weight):
    padded = jnp.concatenate([field_in[:, -1:], field_in, field_in[:, :1]], axis=1)
    result = lax.conv_general_dilated(padded[None], weight, (1, 1), ((1, 1), (0, 0)), dimension_numbers=("NHWC", "HWIO", "NHWC"), preferred_element_type=jnp.float32)
    return result[0]


def flipped(weight):
    return jnp.transpose(weight[::-1, ::-1], (0, 1, 3, 2))


def reference(analysis_vector, prior_estimate, prior_precision, encoder_weight, conv_weights, readout_matrix, obs_in_weight, obs_out_weight, obs_values, obs_precision, foot_cells, obs_count):
    state_half16 = lax.optimization_barrier(analysis_vector.astype(jnp.bfloat16))
    latent_width = jnp.einsum("ojy,om->jym", state_half16.astype(jnp.float32), encoder_weight.astype(jnp.float32)).astype(jnp.bfloat16)
    pre_list = []
    for layer_idx in range(LAYERS):
        pre_act = wrap_conv(latent_width, conv_weights[layer_idx])
        pre_list.append(pre_act)
        latent_width = (latent_width.astype(jnp.float32) + jax.nn.silu(pre_act)).astype(jnp.bfloat16)
    latent_width = lax.optimization_barrier(latent_width)
    predicted_grid = analysis_vector + jnp.einsum("ujw,wk->kuj", latent_width.astype(jnp.float32), readout_matrix.astype(jnp.float32))
    vertical_profiles = lax.optimization_barrier(predicted_grid.reshape(PROGNOSTIC_VARS, MERIDIAN_POINTS * ZONAL_POINTS).astype(jnp.bfloat16))
    block_cells = foot_cells.reshape(TILES, OBS_DEV, FOOT)
    block_values = obs_values.reshape(TILES, OBS_DEV, NCH)
    in_weight = obs_in_weight.astype(jnp.float32)

    def one_block(block_args):
        cell_ids, targets, obs_n = block_args
        gathered = vertical_profiles[:, cell_ids.T].astype(jnp.float32)
        inner_sum = jnp.einsum("vfo,fvh->oh", gathered, in_weight)
        active = jax.nn.silu(inner_sum).astype(jnp.bfloat16)
        predicted = jnp.dot(active, obs_out_weight, preferred_element_type=jnp.float32)
        is_valid = (jnp.arange(OBS_DEV) < obs_n)[:, None]
        departure = jnp.where(is_valid, (predicted - targets) * obs_precision, jnp.zeros((), jnp.float32))
        weighted = (departure * obs_precision).astype(jnp.bfloat16)
        back_act = jnp.dot(weighted, obs_out_weight.T, preferred_element_type=jnp.float32)
        back_inner = lax.optimization_barrier((back_act * silu_slope(inner_sum)).astype(jnp.bfloat16))
        back_cols = jnp.einsum("oh,fvh->vfo", back_inner.astype(jnp.float32), in_weight).astype(jnp.bfloat16)
        return departure, back_cols

    departures, back_all = lax.map(one_block, (block_cells, block_values, obs_count))
    gridpoint_order = block_cells.transpose(0, 2, 1).reshape(-1)
    member_deviation = back_all.transpose(1, 0, 2, 3).reshape(PROGNOSTIC_VARS, -1).astype(jnp.float32)
    prediction_cotangent = jnp.zeros((PROGNOSTIC_VARS, MERIDIAN_POINTS * ZONAL_POINTS), jnp.float32).at[:, gridpoint_order].add(member_deviation)
    prediction_cotangent = prediction_cotangent.reshape(PROGNOSTIC_VARS, MERIDIAN_POINTS, ZONAL_POINTS)
    cotangent_entry = lax.optimization_barrier(prediction_cotangent.astype(jnp.bfloat16))
    adjoint_field = jnp.einsum("erk,me->rkm", cotangent_entry.astype(jnp.float32), readout_matrix.astype(jnp.float32))
    for layer_idx in reversed(range(LAYERS)):
        slope_bf = (adjoint_field * silu_slope(pre_list[layer_idx])).astype(jnp.bfloat16)
        adjoint_field = adjoint_field + wrap_conv(slope_bf, flipped(conv_weights[layer_idx]))
    adjoint_half16 = lax.optimization_barrier(adjoint_field.astype(jnp.bfloat16))
    embedding_result = jnp.einsum("qul,fl->fqu", adjoint_half16.astype(jnp.float32), encoder_weight.astype(jnp.float32))
    cost_derivative = prior_precision[:, None, None] * (analysis_vector - prior_estimate) + prediction_cotangent + embedding_result
    return departures.reshape(OBS_TOTAL, NCH), cost_derivative
```

```python
import functools
import itertools

import jax
import jax.numpy as jnp
from jax import lax
from jax.experimental import pallas as pl
from jax.experimental.pallas import tpu as pltpu
from jax.sharding import PartitionSpec as P

F32 = jnp.float32
BF16 = jnp.bfloat16
LANES = 128
EDGE = 8
HALO = 4
BACK = 2
META = 8
VMEM = pltpu.VMEM
SMEM = pltpu.SMEM


def call(body, outs, n_in, scratch=(), smem=(), flops=0, moved=0, name=None):
    specs = [pl.BlockSpec(memory_space=SMEM if i in smem else VMEM) for i in range(n_in)]
    return pl.pallas_call(
        body,
        out_shape=tuple(jax.ShapeDtypeStruct(s, d) for s, d in outs),
        in_specs=specs,
        out_specs=tuple(pl.BlockSpec(memory_space=VMEM) for _ in outs),
        scratch_shapes=list(scratch),
        cost_estimate=pl.CostEstimate(flops=flops, bytes_accessed=moved, transcendentals=0),
        name=name,
    )


def sigma(v):
    return 0.5 * jnp.tanh(0.5 * v) + 0.5


def dot(a, b):
    return jnp.dot(a, b, preferred_element_type=F32)


def state_body(a_ref, at_ref, s_ref, first_ref, last_ref):
    v, rows, cols = a_ref.shape
    pad = jnp.zeros((LANES - v, cols), F32)
    for r in range(rows):
        x = jnp.concatenate([a_ref[:, r, :], pad], axis=0).T
        at_ref[r] = x
        half = x.astype(BF16)
        s_ref[r] = half
        first_ref[r] = half[:EDGE]
        last_ref[r] = half[cols - EDGE :]


def pack_body(order_ref, obs_ref, meta_ref, out_ref):
    tiles = out_ref.shape[0]
    per = out_ref.shape[1] - META

    def one(p, c):
        h = order_ref[p]
        out_ref[h, 0:per, :] = obs_ref[pl.ds(p, per, stride=tiles), :].astype(BF16)
        return c

    lax.fori_loop(0, tiles, one, 0)
    for h in range(tiles):
        out_ref[h, per : per + META, :] = meta_ref[h]


def unpack_body(order_ref, count_ref, got_ref, obs_ref, prec_ref, out_ref):
    tiles, per, _ = got_ref.shape
    prec = prec_ref[...]
    slot = lax.broadcasted_iota(jnp.int32, (per, LANES), 0) * tiles

    def one(p, c):
        h = order_ref[p]
        obs = obs_ref[pl.ds(p, per, stride=tiles), :]
        dep = (got_ref[h].astype(F32) - obs) * prec
        out_ref[pl.ds(p, per, stride=tiles), :] = jnp.where(slot + p < count_ref[0], dep, 0.0)
        return c

    lax.fori_loop(0, tiles, one, 0)


def shift_pairs(size, wrap):
    up = [(i, (i + 1) % size) for i in range(size if wrap else size - 1)]
    return up, [(j, i) for i, j in up]


def halo(mid, first, last, width):
    up, down = shift_pairs(lax.axis_size("lat"), False)
    rows = mid.shape[0]
    top = lax.ppermute(mid[rows - width :], "lat", up)
    bottom = lax.ppermute(mid[:width], "lat", down)
    up, down = shift_pairs(lax.axis_size("lon"), True)
    cols = mid.shape[1]
    near = jnp.concatenate([top[:, :EDGE], first, bottom[:, :EDGE]], axis=0)
    far = jnp.concatenate([top[:, cols - EDGE :], last, bottom[:, cols - EDGE :]], axis=0)
    left = lax.ppermute(far, "lon", up)
    right = lax.ppermute(near, "lon", down)
    side = jnp.concatenate([right, left], axis=1)
    return top, bottom, side


def row_parts(mid_ref, top_ref, bottom_ref, width):
    rows = mid_ref.shape[0]
    return (
        (width, 0, top_ref),
        (rows, width, mid_ref),
        (width, width + rows, bottom_ref),
    )


def put_shifted(ref, e, value):
    w, ch = value.shape
    ref[e, :, 0:ch] = pltpu.roll(value, 1, 0).astype(BF16)
    ref[e, :, ch : 2 * ch] = value.astype(BF16)
    ref[e, :, 2 * ch : 3 * ch] = pltpu.roll(value, w - 1, 0).astype(BF16)


def conv_rows(ref, e, count, width, weight):
    parts = [
        ref[pl.ds(e + i, count), 0:width, :].reshape(count * width, ref.shape[2]) for i in range(3)
    ]
    return dot(jnp.concatenate(parts, axis=1), weight)


def inside(row0_ref, a):
    g = row0_ref[0] + a
    return jnp.logical_and(g >= 0, g < row0_ref[1])


STEP = 2


def forward_body(
    row0_ref, mid_ref, top_ref, bottom_ref, side_ref, at_ref, enc_ref, w_ref, ro_ref,
    cols_ref, slope0_ref, slope1_ref, a0, a1,
):
    rows, cols, _ = mid_ref.shape
    width, ch = a0.shape[1], enc_ref.shape[1]
    for count, base, src in row_parts(mid_ref, top_ref, bottom_ref, HALO):

        def embed(i, c, base=base, src=src):
            x = jnp.concatenate([src[i], side_ref[base + i]], axis=0)
            h = dot(x, enc_ref[...]).astype(BF16).astype(F32)
            put_shifted(a0, base + i, h)
            return c

        lax.fori_loop(0, count, embed, 0)

    def first(k, c):
        e = k * STEP
        pre = conv_rows(a0, e, STEP, width, w_ref[0]).reshape(STEP, width, ch)
        s = sigma(pre)
        act = pre * s
        slope0_ref[pl.ds(e, STEP)] = (s + act * (1.0 - s)).astype(BF16)
        for q in range(STEP):
            h = a0[e + q + 1, :, ch : 2 * ch].astype(F32) + act[q]
            h = jnp.where(inside(row0_ref, e + q - HALO + 1), h, 0.0)
            put_shifted(a1, e + q, h.astype(BF16).astype(F32))
        return c

    lax.fori_loop(0, (rows + 2 * HALO - 2) // STEP, first, 0)

    def second(k, c):
        e = k * STEP
        pre = conv_rows(a1, e, STEP, width, w_ref[1]).reshape(STEP, width, ch)
        s = sigma(pre)
        act = pre * s
        slope1_ref[pl.ds(e, STEP)] = (s + act * (1.0 - s)).astype(BF16)
        a = e - (HALO - 2)

        @pl.when(jnp.logical_and(a >= 0, a < rows))
        def _():
            for q in range(STEP):
                h = a1[e + q + 1, 0:cols, ch : 2 * ch].astype(F32) + act[q, 0:cols]
                grow = dot(h.astype(BF16), ro_ref[...])
                cols_ref[a + q] = (at_ref[a + q] + grow).astype(BF16)

        return c

    lax.fori_loop(0, (rows + 2 * HALO - 4) // STEP, second, 0)


BLOCK = 512


def observe_body(
    table_ref, cols_ref, got_ref, win_ref, wout_ref, woutt_ref, wint_ref, prec_ref,
    adj_ref, half_ref, pred_ref,
    xs, slope, grid, hot, weights, fa, meta,
):
    rows, cols, _ = cols_ref.shape
    cells = rows * cols
    half = cells // 2
    tiles, per, nch = pred_ref.shape
    obs_n = tiles * per
    group = LANES // per
    prec2 = prec_ref[...] * prec_ref[...]
    c0 = cols_ref[...].reshape(cells, LANES)
    c1 = pltpu.roll(c0.astype(F32), cells - 1, 0).astype(BF16)
    xs[0] = c0
    xs[1] = c1
    xs[2] = jnp.concatenate([c0[cols:], c0[:cols]], axis=0)
    xs[3] = jnp.concatenate([c1[cols:], c1[:cols]], axis=0)
    rest = jnp.zeros((1, LANES), F32)
    for m in range(obs_n // LANES):
        total = got_ref[m * group, per : per + META, :].astype(F32)
        for g in range(1, group):
            total += got_ref[m * group + g, per : per + META, :].astype(F32)
        meta[m] = total
        rest += jnp.where(total[2:3] == table_ref[0, 4].astype(F32), 0.0, 1.0)
    trips = jnp.where(jnp.sum(rest) > 0.0, table_ref.shape[0], 1)
    fa[...] = jnp.zeros_like(fa)

    def arrangement(cls, carry):
        place = [table_ref[cls, f] for f in range(4)]
        code = table_ref[cls, 4].astype(F32)

        def forward(k, c):
            at = pl.ds(k * BLOCK, BLOCK)
            x = jnp.concatenate([xs[place[f], at, :] for f in range(4)], axis=1)
            inner = dot(x, win_ref[...])
            s = sigma(inner)
            act = inner * s
            slope[at, :] = (s + act * (1.0 - s)).astype(BF16)
            grid[at, :] = dot(act.astype(BF16), wout_ref[...]).astype(BF16)
            return c

        lax.fori_loop(0, cells // BLOCK, forward, 0)
        both = jnp.concatenate([grid[0:half, :], grid[half:, :]], axis=1)
        lane = lax.broadcasted_iota(jnp.int32, (LANES, LANES), 1).astype(F32)
        sub = lax.broadcasted_iota(jnp.int32, (LANES, LANES), 0).astype(F32)
        top = float(rows // 2)

        def gather(m, c):
            mine = meta[m, 2:3, :] == code
            row = jnp.broadcast_to(jnp.where(mine, meta[m, 0:1, :], float(rows)), (LANES, LANES))
            col = jnp.broadcast_to(meta[m, 1:2, :], (LANES, LANES))
            row_t, col_t = row.T, col.T
            local = jnp.where(row_t < top, row_t, row_t - top)
            value = jnp.where(col_t == lane, local, -1.0)
            sel = jnp.concatenate(
                [jnp.where(value == float(t), 1.0, 0.0).astype(BF16) for t in range(rows // 2)],
                axis=1,
            )
            out = dot(sel, both)
            upper = row_t >= top
            pred = jnp.where(upper, out[:, nch:], out[:, :nch])
            pred = jnp.where(row_t < float(rows), pred, 0.0)
            obs = got_ref[pl.ds(m * group, group), 0:per, :].astype(F32).reshape(LANES, nch)
            w = (pred - obs) * prec2
            at = pl.ds(m * LANES, LANES)
            weights[at, 0:nch] = jnp.where(upper, 0.0, w).astype(BF16)
            weights[at, nch:] = jnp.where(upper, w, 0.0).astype(BF16)
            pred = pred.reshape(group, per, nch)
            where = pl.ds(m * group, group)

            @pl.when(cls == 0)
            def _():
                pred_ref[where] = pred.astype(BF16)

            @pl.when(cls > 0)
            def _():
                pred_ref[where] = (pred_ref[where].astype(F32) + pred).astype(BF16)

            local = jnp.where(row < top, row, row - top)
            value = jnp.where(col == sub, local, -1.0)
            for t in range(rows // 2):
                hot[t * LANES : (t + 1) * LANES, pl.ds(pl.multiple_of(m * LANES, LANES), LANES)] = (
                    jnp.where(value == float(t), 1.0, 0.0).astype(BF16)
                )
            return c

        lax.fori_loop(0, obs_n // LANES, gather, 0)

        def scatter(k, c):
            at = pl.ds(k * BLOCK, BLOCK)
            total = dot(hot[at, :], weights[...])
            grid[at, :] = total[:, :nch].astype(BF16)
            grid[pl.ds(half + k * BLOCK, BLOCK), :] = total[:, nch:].astype(BF16)
            return c

        lax.fori_loop(0, half // BLOCK, scatter, 0)

        def backward(k, c):
            at = pl.ds(k * BLOCK, BLOCK)
            act = dot(grid[at, :], woutt_ref[...])
            inner = (act * slope[at, :].astype(F32)).astype(BF16)
            x = dot(inner, wint_ref[...])
            for f in range(4):
                fa[place[f], at, :] += x[:, f * LANES : (f + 1) * LANES]
            return c

        lax.fori_loop(0, cells // BLOCK, backward, 0)
        return carry

    lax.fori_loop(0, trips, arrangement, 0)
    high = fa[3]
    one = fa[1] + jnp.concatenate([high[cells - cols :], high[: cells - cols]], axis=0)
    low = fa[2]
    total = fa[0] + jnp.concatenate([low[cells - cols :], low[: cells - cols]], axis=0)
    total += pltpu.roll(one, 1, 0)
    total = total.reshape(rows, cols, LANES)
    adj_ref[...] = total
    half_ref[...] = total.astype(BF16)


def adjoint_body(
    row0_ref, mid_ref, top_ref, bottom_ref, side_ref, adj_ref, slope0_ref, slope1_ref,
    rot_ref, w_ref, enct_ref, state_ref, prior_ref, prec_ref,
    out_ref, b1, b0, adj2, adj1,
):
    rows, cols, _ = mid_ref.shape
    width, ch = b1.shape[1], rot_ref.shape[1]
    v = out_ref.shape[0]
    for count, base, src in row_parts(mid_ref, top_ref, bottom_ref, BACK):

        def lift(i, c, base=base, src=src):
            x = jnp.concatenate([src[i], side_ref[base + i]], axis=0)
            g = dot(x, rot_ref[...])
            adj2[base + i] = g
            g = (g * slope1_ref[base + i].astype(F32)).astype(BF16)
            put_shifted(b1, base + i, g.astype(F32))
            return c

        lax.fori_loop(0, count, lift, 0)

    def first(k, c):
        e = k * STEP
        g = conv_rows(b1, e, STEP, width, w_ref[1]).reshape(STEP, width, ch)
        for q in range(STEP):
            total = adj2[e + q + 1] + g[q]
            adj1[e + q] = total
            h = total * slope0_ref[e + q + 2].astype(F32)
            h = jnp.where(inside(row0_ref, e + q - 1), h, 0.0)
            put_shifted(b0, e + q, h.astype(BF16).astype(F32))
        return c

    lax.fori_loop(0, (rows + 2) // STEP, first, 0)

    def second(k, c):
        a = k * STEP
        g = conv_rows(b0, a, STEP, cols, w_ref[0]).reshape(STEP, cols, ch)
        for q in range(STEP):
            total = adj1[a + q + 1, 0:cols, :] + g[q]
            grow = dot(total.astype(BF16), enct_ref[...]) + adj_ref[a + q]
            diff = state_ref[:, a + q, :] - prior_ref[:, a + q, :]
            out_ref[:, a + q, :] = prec_ref[...] * diff + grow.T[0:v, :]
        return c

    lax.fori_loop(0, rows // STEP, second, 0)


def arrangement_table():
    orders = list(itertools.permutations(range(4)))
    first = (0, 2, 1, 3)
    orders.remove(first)
    return [
        list(o) + [sum(q * 4**f for f, q in enumerate(o))] for o in [first] + orders
    ]


def on_device(
    analysis_vector,
    prior_estimate,
    prior_precision,
    encoder_weight,
    conv_weights,
    readout_matrix,
    obs_in_weight,
    obs_out_weight,
    obs_values,
    obs_precision,
    foot_cells,
    obs_count,
):
    v, rows, cols = analysis_vector.shape
    n_lat, n_lon = lax.axis_size("lat"), lax.axis_size("lon")
    tiles = n_lat * n_lon
    obs_n, foot = foot_cells.shape
    per = obs_n // tiles
    ch = encoder_weight.shape[1]
    hid, nch = obs_out_weight.shape
    width = cols + 2 * EDGE
    cells = rows * cols
    lat, lon = lax.axis_index("lat"), lax.axis_index("lon")
    row0 = jnp.stack([lat * rows, jnp.int32(n_lat * rows)])

    at, s16, first, last = call(
        state_body,
        [((rows, cols, LANES), F32), ((rows, cols, LANES), BF16)] + [((rows, EDGE, LANES), BF16)] * 2,
        1, moved=cells * v * 8, name="state",
    )(analysis_vector)
    top, bottom, side = halo(s16, first, last, HALO)

    lon_total = cols * n_lon
    lat_g, lon_g = foot_cells // lon_total, foot_cells % lon_total
    order = lat_g[:tiles, 0] // rows * n_lon + lon_g[:tiles, 0] // cols
    base_lat, base_lon = jnp.min(lat_g, axis=1), jnp.min(lon_g, axis=1)
    place = (lat_g - base_lat[:, None]) * 2 + (lon_g - base_lon[:, None])
    code = jnp.sum(place * (4 ** jnp.arange(foot)), axis=1)
    valid = jnp.arange(obs_n) < obs_count[0]
    local = jnp.where(valid, base_lat % rows, rows)
    fields = jnp.stack([local, base_lon % cols, code]).astype(BF16).reshape(3, per, tiles)
    pick = (order[None, :] == jnp.arange(tiles)[:, None]).astype(BF16)
    meta = jnp.einsum("fkp,hp->hfk", fields, pick, preferred_element_type=F32).astype(BF16)
    group = LANES // per
    mine = jnp.arange(group) == (lat * n_lon + lon) % group
    meta = jnp.where(mine[:, None], meta[:, :, None, :], jnp.zeros((), BF16)).reshape(tiles, 3, LANES)
    meta = jnp.pad(meta, ((0, 0), (0, META - 3), (0, 0)))
    (send,) = call(
        pack_body, [((tiles, per + META, nch), BF16)], 3, smem=(0,), moved=obs_n * nch * 6, name="pack"
    )(order, obs_values, meta)
    got = lax.all_to_all(send, ("lat", "lon"), split_axis=0, concat_axis=0, tiled=True)

    pad_v = ((0, LANES - v), (0, 0))
    enc = jnp.pad(encoder_weight, pad_v)
    rot = jnp.pad(readout_matrix.T, pad_v)
    win = jnp.pad(obs_in_weight, ((0, 0),) + pad_v).reshape(foot * LANES, hid)
    w_fwd = conv_weights.reshape(conv_weights.shape[0], 9 * ch, ch)
    w_back = jnp.transpose(conv_weights[:, ::-1, ::-1], (0, 1, 2, 4, 3)).reshape(w_fwd.shape)

    conv_flops = 2 * cells * 9 * ch * ch
    cols16, slope0, slope1 = call(
        forward_body,
        [
            ((rows, cols, LANES), BF16),
            ((rows + 2 * HALO - 2, width, ch), BF16),
            ((rows + 2 * HALO - 4, width, ch), BF16),
        ],
        9,
        [VMEM((rows + 2 * HALO, width, 3 * ch), BF16), VMEM((rows + 2 * HALO - 2, width, 3 * ch), BF16)],
        (0,), 3 * conv_flops, cells * ch * 8, "forward",
    )(row0, s16, top, bottom, side, at, enc, w_fwd, rot.T)

    adj, adj16, pred = call(
        observe_body,
        [((rows, cols, LANES), F32), ((rows, cols, LANES), BF16), ((tiles, per, nch), BF16)],
        8,
        [
            VMEM((4, cells, LANES), BF16),
            VMEM((cells, hid), BF16),
            VMEM((cells, nch), BF16),
            VMEM((cells // 2, obs_n), BF16),
            VMEM((obs_n, 2 * nch), BF16),
            VMEM((4, cells, LANES), F32),
            VMEM((obs_n // LANES, META, LANES), F32),
        ],
        (0,), 4 * cells * hid * (foot * LANES + nch), cells * hid * 4, "observe",
    )(
        jnp.array(arrangement_table(), jnp.int32), cols16, got, win, obs_out_weight,
        obs_out_weight.T, win.T, obs_precision[None, :],
    )
    back = lax.all_to_all(pred, ("lat", "lon"), split_axis=0, concat_axis=0, tiled=True)

    top, bottom, side = halo(adj16, adj16[:, :EDGE], adj16[:, cols - EDGE :], BACK)
    (derivative,) = call(
        adjoint_body,
        [((v, rows, cols), F32)],
        14,
        [
            VMEM((rows + 2 * BACK, width, 3 * ch), BF16),
            VMEM((rows + 2, width, 3 * ch), BF16),
            VMEM((rows + 2 * BACK, width, ch), F32),
            VMEM((rows + 2, width, ch), F32),
        ],
        (0,), 3 * conv_flops, cells * ch * 8, "adjoint",
    )(
        row0, adj16, top, bottom, side, adj, slope0, slope1, rot, w_back, enc.T,
        analysis_vector, prior_estimate, jnp.broadcast_to(prior_precision[:, None], (v, cols)),
    )
    (departures,) = call(
        unpack_body, [((obs_n, nch), F32)], 5, smem=(0, 1), moved=obs_n * nch * 10, name="unpack"
    )(order, obs_count, back, obs_values, obs_precision[None, :])
    return departures, derivative


def solution(mesh):
    return jax.shard_map(
        on_device,
        mesh=mesh,
        in_specs=(
            P(None, "lat", "lon"),
            P(None, "lat", "lon"),
            P(),
            P(),
            P(),
            P(),
            P(),
            P(),
            P(("lat", "lon"), None),
            P(),
            P(("lat", "lon"), None),
            P(("lat", "lon")),
        ),
        out_specs=(P(("lat", "lon"), None), P(None, "lat", "lon")),
        check_vma=False,
    )
```

```python
import functools
import itertools

import jax
import jax.numpy as jnp
from jax import lax
from jax.experimental import pallas as pl
from jax.experimental.pallas import tpu as pltpu
from jax.sharding import PartitionSpec as P

F32 = jnp.float32
BF16 = jnp.bfloat16
LANES = 128
EDGE = 8
HALO = 4
BACK = 2
META = 8
VMEM = pltpu.VMEM
SMEM = pltpu.SMEM


def call(body, outs, n_in, scratch=(), smem=(), flops=0, moved=0, name=None, limit=16):
    specs = [pl.BlockSpec(memory_space=SMEM if i in smem else VMEM) for i in range(n_in)]
    return pl.pallas_call(
        body,
        out_shape=tuple(jax.ShapeDtypeStruct(s, d) for s, d in outs),
        in_specs=specs,
        out_specs=tuple(pl.BlockSpec(memory_space=VMEM) for _ in outs),
        scratch_shapes=list(scratch),
        cost_estimate=pl.CostEstimate(flops=flops, bytes_accessed=moved, transcendentals=0),
        compiler_params=pltpu.CompilerParams(vmem_limit_bytes=limit * 2**20),
        name=name,
    )


def sigma(v):
    return 0.5 * jnp.tanh(0.5 * v) + 0.5


def dot(a, b):
    return jnp.dot(a, b, preferred_element_type=F32)


def dot_t(a, b):
    return lax.dot_general(a, b, (((1,), (1,)), ((), ())), preferred_element_type=F32)


def padded(ref, src_ref):
    ref[...] = jnp.zeros_like(ref)
    ref[0 : src_ref.shape[0], :] = src_ref[...]


def edges(half, r, rows, width, first_ref, last_ref, head_ref, tail_ref):
    first_ref[r] = half[:EDGE]
    last_ref[r] = half[half.shape[0] - EDGE :]
    if r < width:
        head_ref[r] = half
    if r >= rows - width:
        tail_ref[r - rows + width] = half


def state_body(a_ref, at_ref, s_ref, first_ref, last_ref, head_ref, tail_ref):
    v, rows, cols = a_ref.shape
    pad = jnp.zeros((LANES - v, cols), F32)
    for r in range(rows):
        x = jnp.concatenate([a_ref[:, r, :], pad], axis=0).T
        at_ref[r] = x
        half = x.astype(BF16)
        s_ref[r] = half
        edges(half, r, rows, HALO, first_ref, last_ref, head_ref, tail_ref)


def sides_body(top_ref, bottom_ref, first_ref, last_ref, near_ref, far_ref):
    width, cols, _ = top_ref.shape
    rows = first_ref.shape[0]
    near_ref[0:width] = top_ref[:, :EDGE]
    near_ref[width : width + rows] = first_ref[...]
    near_ref[width + rows :] = bottom_ref[:, :EDGE]
    far_ref[0:width] = top_ref[:, cols - EDGE :]
    far_ref[width : width + rows] = last_ref[...]
    far_ref[width + rows :] = bottom_ref[:, cols - EDGE :]


def pack_body(order_ref, obs_ref, meta_ref, out_ref):
    tiles = out_ref.shape[0]
    per = out_ref.shape[1] - META

    def one(p, c):
        h = order_ref[p]
        out_ref[h, 0:per, :] = obs_ref[pl.ds(p, per, stride=tiles), :].astype(BF16)
        return c

    lax.fori_loop(0, tiles, one, 0)
    for h in range(tiles):
        out_ref[h, per : per + META, :] = meta_ref[h]


def unpack_body(order_ref, count_ref, got_ref, obs_ref, prec_ref, out_ref):
    tiles, per, _ = got_ref.shape
    prec = prec_ref[...]
    slot = lax.broadcasted_iota(jnp.int32, (per, LANES), 0) * tiles

    def one(p, c):
        h = order_ref[p]
        obs = obs_ref[pl.ds(p, per, stride=tiles), :]
        dep = (got_ref[h].astype(F32) - obs) * prec
        out_ref[pl.ds(p, per, stride=tiles), :] = jnp.where(slot + p < count_ref[0], dep, 0.0)
        return c

    lax.fori_loop(0, tiles, one, 0)


def shift_pairs(size, wrap):
    up = [(i, (i + 1) % size) for i in range(size if wrap else size - 1)]
    return up, [(j, i) for i, j in up]


def halo(first, last, head, tail, after=None):
    up, down = shift_pairs(lax.axis_size("lat"), False)
    top = lax.ppermute(tail, "lat", up)
    bottom = lax.ppermute(head, "lat", down)
    up, down = shift_pairs(lax.axis_size("lon"), True)
    shape = (first.shape[0] + 2 * head.shape[0],) + first.shape[1:]
    near, far = call(sides_body, [(shape, BF16)] * 2, 4, name="sides", limit=4)(
        top, bottom, first, last
    )
    left = lax.ppermute(far, "lon", up)
    right = lax.ppermute(near, "lon", down)
    return top, bottom, right, left


def bands(mid_ref, top_ref, bottom_ref, width):
    rows = mid_ref.shape[0]
    return (
        [(top_ref, r) for r in range(width)]
        + [(mid_ref, r) for r in range(rows)]
        + [(bottom_ref, r) for r in range(width)]
    )


def fold_row(nat_ref, e, q_n):
    slabs = [nat_ref[e, pl.ds(q, SUB, stride=q_n), :] for q in range(q_n)]
    return jnp.concatenate(slabs, axis=0)


def unfold_row(nat_ref, e, value, q_n):
    for q in range(q_n):
        nat_ref[e, pl.ds(q, SUB, stride=q_n), :] = value[q * SUB : (q + 1) * SUB]


def put_row(ref, e, value):
    n, ch = value.shape
    q_n = n // SUB
    ref[e, 1 : q_n + 1] = value.astype(BF16).reshape(q_n, SUB, ch)
    ref[e, 0] = pltpu.roll(value[n - SUB :], 1, 0).astype(BF16)
    ref[e, q_n + 1] = pltpu.roll(value[:SUB], SUB - 1, 0).astype(BF16)


def center(ref, e):
    q_n, ch = ref.shape[1] - 2, ref.shape[3]
    return ref[e, 1 : q_n + 1].reshape(q_n * SUB, ch)


def conv_rows(ref, e, count, weight):
    q_n, ch = ref.shape[1] - 2, ref.shape[3]
    parts = [
        ref[e + i : e + i + count, j : j + q_n].reshape(count * q_n * SUB, ch)
        for i in range(3)
        for j in range(3)
    ]
    return dot(jnp.concatenate(parts, axis=1), weight)


def inside(lat_ref, a, rows, n_lat):
    g = lat_ref[0] * rows + a
    return jnp.logical_and(g >= 0, g < n_lat * rows)


STEP = 2
SUB = 16


def forward_body(
    n_lat, lat_ref, mid_ref, top_ref, bottom_ref, right_ref, left_ref, at_ref, enc_in, w_ref, ro_in,
    cols_ref, slope0_ref, slope1_ref, a0, a1, nat, back, enc_ref, ro_ref,
):
    padded(enc_ref, enc_in)
    padded(ro_ref, ro_in)
    rows, cols, _ = mid_ref.shape
    q_n = a0.shape[1] - 2
    n = q_n * SUB
    for e, (src, r) in enumerate(bands(mid_ref, top_ref, bottom_ref, HALO)):
        nat[e, 0:cols, :] = src[r].astype(F32)
        nat[e, cols : cols + EDGE, :] = right_ref[e].astype(F32)
        nat[e, cols + EDGE :, :] = left_ref[e].astype(F32)
        x = fold_row(nat, e, q_n).astype(BF16)
        put_row(a0, e, dot(x, enc_ref[...]))

    def first(e):
        pre = conv_rows(a0, e, STEP, w_ref[0])
        s = sigma(pre)
        act = pre * s
        slope = (s + act * (1.0 - s)).astype(BF16)
        for q in range(STEP):
            at = slice(q * n, (q + 1) * n)
            slope0_ref[e + q] = slope[at]
            h = center(a0, e + q + 1).astype(F32) + act[at]
            a = e + q - HALO + 1
            if a < 0 or a >= rows:
                h = jnp.where(inside(lat_ref, a, rows, n_lat), h, 0.0)
            put_row(a1, e + q, h)

    def second(e):
        pre = conv_rows(a1, e, STEP, w_ref[1])
        s = sigma(pre)
        act = pre * s
        slope = (s + act * (1.0 - s)).astype(BF16)
        for q in range(STEP):
            at = slice(q * n, (q + 1) * n)
            slope1_ref[e + q] = slope[at]
            a = e + q - HALO + 2
            if 0 <= a < rows:
                h = center(a1, e + q + 1).astype(F32) + act[at]
                unfold_row(back, a, dot_t(h.astype(BF16), ro_ref[...]), q_n)
                cols_ref[a] = (at_ref[a] + back[a, 0:cols, :]).astype(BF16)

    for e in range(0, rows + 2 * HALO - 2, STEP):
        first(e)
    for e in range(0, rows + 2 * HALO - 4, STEP):
        second(e)


def adjoint_body(
    n_lat, lat_ref, mid_ref, top_ref, bottom_ref, right_ref, left_ref, adj_ref, slope0_ref, slope1_ref,
    rot_in, w_ref, enc_in, state_ref, prior_ref, prec_in,
    out_ref, b1, b0, adj2, adj1, nat, back, rot_ref, enc_ref, prec_pad,
):
    padded(rot_ref, rot_in)
    padded(enc_ref, enc_in)
    prec_pad[...] = jnp.zeros_like(prec_pad)
    prec_pad[0:1, 0 : prec_in.shape[1]] = prec_in[...]
    rows, cols, _ = mid_ref.shape
    q_n = b1.shape[1] - 2
    n = q_n * SUB
    v = out_ref.shape[0]
    prec = jnp.broadcast_to(prec_pad[0:1, :], (LANES, LANES)).T[0:v, :]
    for e, (src, r) in enumerate(bands(mid_ref, top_ref, bottom_ref, BACK)):
        nat[e, 0:cols, :] = src[r].astype(F32)
        nat[e, cols : cols + EDGE, :] = right_ref[e].astype(F32)
        nat[e, cols + EDGE :, :] = left_ref[e].astype(F32)
        g = dot(fold_row(nat, e, q_n).astype(BF16), rot_ref[...])
        adj2[e] = g
        put_row(b1, e, g * slope1_ref[e].astype(F32))

    for e in range(0, rows + 2, STEP):
        g = conv_rows(b1, e, STEP, w_ref[1])
        for q in range(STEP):
            total = adj2[e + q + 1] + g[q * n : (q + 1) * n]
            adj1[e + q] = total
            h = total * slope0_ref[e + q + 2].astype(F32)
            a = e + q - 1
            if a < 0 or a >= rows:
                h = jnp.where(inside(lat_ref, a, rows, n_lat), h, 0.0)
            put_row(b0, e + q, h)

    for a in range(0, rows, STEP):
        g = conv_rows(b0, a, STEP, w_ref[0])
        for q in range(STEP):
            total = adj1[a + q + 1] + g[q * n : (q + 1) * n]
            unfold_row(back, a + q, dot_t(total.astype(BF16), enc_ref[...]), q_n)
            grow = back[a + q, 0:cols, :] + adj_ref[a + q]
            diff = state_ref[:, a + q, :] - prior_ref[:, a + q, :]
            out_ref[:, a + q, :] = prec * diff + grow.T[0:v, :]


BLOCK = 512


def observe_body(
    table_ref, cols_ref, got_ref, win_ref, wout_ref, prec_ref,
    adj_ref, half_ref, first_ref, last_ref, head_ref, tail_ref, pred_ref,
    xs, slope, grid, hot, weights, fa, meta,
):
    rows, cols, _ = cols_ref.shape
    cells = rows * cols
    half = cells // 2
    tiles, per, nch = pred_ref.shape
    obs_n = tiles * per
    group = LANES // per
    prec2 = prec_ref[...] * prec_ref[...]
    c0 = cols_ref[...].reshape(cells, LANES)
    c1 = pltpu.roll(c0.astype(F32), cells - 1, 0).astype(BF16)
    xs[0] = c0
    xs[1] = c1
    xs[2] = jnp.concatenate([c0[cols:], c0[:cols]], axis=0)
    xs[3] = jnp.concatenate([c1[cols:], c1[:cols]], axis=0)
    rest = jnp.zeros((1, LANES), F32)
    for m in range(obs_n // LANES):
        total = got_ref[m * group, per : per + META, :].astype(F32)
        for g in range(1, group):
            total += got_ref[m * group + g, per : per + META, :].astype(F32)
        meta[m] = total
        rest += jnp.where(total[2:3] == table_ref[0, 4].astype(F32), 0.0, 1.0)
    trips = jnp.where(jnp.sum(rest) > 0.0, table_ref.shape[0], 1)
    fa[...] = jnp.zeros_like(fa)

    def arrangement(cls, carry):
        place = [table_ref[cls, f] for f in range(4)]
        code = table_ref[cls, 4].astype(F32)

        def forward(k, c):
            at = pl.ds(k * BLOCK, BLOCK)
            x = jnp.concatenate([xs[place[f], at, :] for f in range(4)], axis=1)
            inner = dot(x, win_ref[...])
            s = sigma(inner)
            act = inner * s
            slope[at, :] = (s + act * (1.0 - s)).astype(BF16)
            grid[at, :] = dot(act.astype(BF16), wout_ref[...]).astype(BF16)
            return c

        lax.fori_loop(0, cells // BLOCK, forward, 0)
        both = jnp.concatenate([grid[0:half, :], grid[half:, :]], axis=1)
        lane = lax.broadcasted_iota(jnp.int32, (LANES, LANES), 1).astype(F32)
        sub = lax.broadcasted_iota(jnp.int32, (LANES, LANES), 0).astype(F32)
        top = float(rows // 2)

        def gather(m, c):
            mine = meta[m, 2:3, :] == code
            row = jnp.broadcast_to(jnp.where(mine, meta[m, 0:1, :], float(rows)), (LANES, LANES))
            col = jnp.broadcast_to(meta[m, 1:2, :], (LANES, LANES))
            row_t, col_t = row.T, col.T
            local = jnp.where(row_t < top, row_t, row_t - top)
            value = jnp.where(col_t == lane, local, -1.0)
            sel = jnp.concatenate(
                [jnp.where(value == float(t), 1.0, 0.0).astype(BF16) for t in range(rows // 2)],
                axis=1,
            )
            out = dot(sel, both)
            upper = row_t >= top
            pred = jnp.where(upper, out[:, nch:], out[:, :nch])
            pred = jnp.where(row_t < float(rows), pred, 0.0)
            obs = got_ref[pl.ds(m * group, group), 0:per, :].astype(F32).reshape(LANES, nch)
            w = (pred - obs) * prec2
            at = pl.ds(m * LANES, LANES)
            weights[at, 0:nch] = jnp.where(upper, 0.0, w).astype(BF16)
            weights[at, nch:] = jnp.where(upper, w, 0.0).astype(BF16)
            pred = pred.reshape(group, per, nch)
            where = pl.ds(m * group, group)

            @pl.when(cls == 0)
            def _():
                pred_ref[where] = pred.astype(BF16)

            @pl.when(cls > 0)
            def _():
                pred_ref[where] = (pred_ref[where].astype(F32) + pred).astype(BF16)

            local = jnp.where(row < top, row, row - top)
            value = jnp.where(col == sub, local, -1.0)
            for t in range(rows // 2):
                hot[t * LANES : (t + 1) * LANES, pl.ds(pl.multiple_of(m * LANES, LANES), LANES)] = (
                    jnp.where(value == float(t), 1.0, 0.0).astype(BF16)
                )
            return c

        lax.fori_loop(0, obs_n // LANES, gather, 0)

        def scatter(k, c):
            at = pl.ds(k * BLOCK, BLOCK)
            total = dot(hot[at, :], weights[...])
            grid[at, :] = total[:, :nch].astype(BF16)
            grid[pl.ds(half + k * BLOCK, BLOCK), :] = total[:, nch:].astype(BF16)
            return c

        lax.fori_loop(0, half // BLOCK, scatter, 0)

        def backward(k, c):
            at = pl.ds(k * BLOCK, BLOCK)
            act = dot_t(grid[at, :], wout_ref[...])
            inner = (act * slope[at, :].astype(F32)).astype(BF16)
            x = dot_t(inner, win_ref[...])
            for f in range(4):
                fa[place[f], at, :] += x[:, f * LANES : (f + 1) * LANES]
            return c

        lax.fori_loop(0, cells // BLOCK, backward, 0)
        return carry

    lax.fori_loop(0, trips, arrangement, 0)
    high = fa[3]
    one = fa[1] + jnp.concatenate([high[cells - cols :], high[: cells - cols]], axis=0)
    low = fa[2]
    total = fa[0] + jnp.concatenate([low[cells - cols :], low[: cells - cols]], axis=0)
    total += pltpu.roll(one, 1, 0)
    total = total.reshape(rows, cols, LANES)
    adj_ref[...] = total
    total = total.astype(BF16)
    half_ref[...] = total
    for r in range(rows):
        edges(total[r], r, rows, BACK, first_ref, last_ref, head_ref, tail_ref)


def arrangement_table():
    orders = list(itertools.permutations(range(4)))
    first = (0, 2, 1, 3)
    orders.remove(first)
    return [
        list(o) + [sum(q * 4**f for f, q in enumerate(o))] for o in [first] + orders
    ]


def on_device(
    analysis_vector,
    prior_estimate,
    prior_precision,
    encoder_weight,
    conv_weights,
    readout_matrix,
    obs_in_weight,
    obs_out_weight,
    obs_values,
    obs_precision,
    foot_cells,
    obs_count,
):
    v, rows, cols = analysis_vector.shape
    n_lat, n_lon = lax.axis_size("lat"), lax.axis_size("lon")
    tiles = n_lat * n_lon
    obs_n, foot = foot_cells.shape
    per = obs_n // tiles
    ch = encoder_weight.shape[1]
    hid, nch = obs_out_weight.shape
    width = cols + 2 * EDGE
    cells = rows * cols
    lat, lon = lax.axis_index("lat"), lax.axis_index("lon")
    lat_id = lat.reshape(1)

    strip = (rows, EDGE, LANES)
    at, s16, *rim = call(
        state_body,
        [((rows, cols, LANES), F32), ((rows, cols, LANES), BF16)]
        + [(strip, BF16)] * 2 + [((HALO, cols, LANES), BF16)] * 2,
        1, moved=cells * v * 8, name="state",
    )(analysis_vector)
    top, bottom, right, left = halo(*rim)

    lon_total = cols * n_lon
    lat_g, lon_g = foot_cells // lon_total, foot_cells % lon_total
    order = lat_g[:tiles, 0] // rows * n_lon + lon_g[:tiles, 0] // cols
    base_lat, base_lon = jnp.min(lat_g, axis=1), jnp.min(lon_g, axis=1)
    place = (lat_g - base_lat[:, None]) * 2 + (lon_g - base_lon[:, None])
    code = jnp.sum(place * (4 ** jnp.arange(foot)), axis=1)
    valid = jnp.arange(obs_n) < obs_count[0]
    local = jnp.where(valid, base_lat % rows, rows)
    fields = jnp.stack([local, base_lon % cols, code]).astype(BF16).reshape(3, per, tiles)
    pick = (order[None, :] == jnp.arange(tiles)[:, None]).astype(BF16)
    meta = jnp.einsum("fkp,hp->hfk", fields, pick, preferred_element_type=F32).astype(BF16)
    group = LANES // per
    mine = jnp.arange(group) == (lat * n_lon + lon) % group
    meta = jnp.where(mine[:, None], meta[:, :, None, :], jnp.zeros((), BF16)).reshape(tiles, 3, LANES)
    meta = jnp.pad(meta, ((0, 0), (0, META - 3), (0, 0)))
    (send,) = call(
        pack_body, [((tiles, per + META, nch), BF16)], 3, smem=(0,), moved=obs_n * nch * 6, name="pack"
    )(order, obs_values, meta)
    got = lax.all_to_all(send, ("lat", "lon"), split_axis=0, concat_axis=0, tiled=True)

    rot = readout_matrix.T
    win = jnp.pad(obs_in_weight, ((0, 0), (0, LANES - v), (0, 0))).reshape(foot * LANES, hid)
    w_fwd = conv_weights.reshape(conv_weights.shape[0], 9 * ch, ch)
    w_back = jnp.transpose(conv_weights[:, ::-1, ::-1], (0, 1, 2, 4, 3)).reshape(w_fwd.shape)

    conv_flops = 2 * cells * 9 * ch * ch
    cols16, slope0, slope1 = call(
        functools.partial(forward_body, n_lat),
        [
            ((rows, cols, LANES), BF16),
            ((rows + 2 * HALO - 2, width, ch), BF16),
            ((rows + 2 * HALO - 4, width, ch), BF16),
        ],
        10,
        [
            VMEM((rows + 2 * HALO, width // SUB + 2, SUB, ch), BF16),
            VMEM((rows + 2 * HALO - 2, width // SUB + 2, SUB, ch), BF16),
            VMEM((rows + 2 * HALO, width, LANES), F32),
            VMEM((rows, width, LANES), F32),
            VMEM((LANES, ch), BF16),
            VMEM((LANES, ch), BF16),
        ],
        (0,), 3 * conv_flops, cells * ch * 8, "forward", 30,
    )(lat_id, s16, top, bottom, right, left, at, encoder_weight, w_fwd, rot)

    adj, adj16, *rim, pred = call(
        observe_body,
        [((rows, cols, LANES), F32), ((rows, cols, LANES), BF16)]
        + [(strip, BF16)] * 2 + [((BACK, cols, LANES), BF16)] * 2 + [((tiles, per, nch), BF16)],
        6,
        [
            VMEM((4, cells, LANES), BF16),
            VMEM((cells, hid), BF16),
            VMEM((cells, nch), BF16),
            VMEM((cells // 2, obs_n), BF16),
            VMEM((obs_n, 2 * nch), BF16),
            VMEM((4, cells, LANES), F32),
            VMEM((obs_n // LANES, META, LANES), F32),
        ],
        (0,), 4 * cells * hid * (foot * LANES + nch), cells * hid * 4, "observe", 32,
    )(
        jnp.array(arrangement_table(), jnp.int32), cols16, got, win, obs_out_weight,
        obs_precision[None, :],
    )
    back = lax.all_to_all(pred, ("lat", "lon"), split_axis=0, concat_axis=0, tiled=True)

    top, bottom, right, left = halo(*rim)
    (derivative,) = call(
        functools.partial(adjoint_body, n_lat),
        [((v, rows, cols), F32)],
        15,
        [
            VMEM((rows + 2 * BACK, width // SUB + 2, SUB, ch), BF16),
            VMEM((rows + 2, width // SUB + 2, SUB, ch), BF16),
            VMEM((rows + 2 * BACK, width, ch), F32),
            VMEM((rows + 2, width, ch), F32),
            VMEM((rows + 2 * BACK, width, LANES), F32),
            VMEM((rows, width, LANES), F32),
            VMEM((LANES, ch), BF16),
            VMEM((LANES, ch), BF16),
            VMEM((8, LANES), F32),
        ],
        (0,), 3 * conv_flops, cells * ch * 8, "adjoint", 34,
    )(
        lat_id, adj16, top, bottom, right, left, adj, slope0, slope1, rot, w_back, encoder_weight,
        analysis_vector, prior_estimate, prior_precision[None, :],
    )
    (departures,) = call(
        unpack_body, [((obs_n, nch), F32)], 5, smem=(0, 1), moved=obs_n * nch * 10, name="unpack"
    )(order, obs_count, back, obs_values, obs_precision[None, :])
    return departures, derivative


def solution(mesh):
    return jax.shard_map(
        on_device,
        mesh=mesh,
        in_specs=(
            P(None, "lat", "lon"),
            P(None, "lat", "lon"),
            P(),
            P(),
            P(),
            P(),
            P(),
            P(),
            P(("lat", "lon"), None),
            P(),
            P(("lat", "lon"), None),
            P(("lat", "lon")),
        ),
        out_specs=(P(("lat", "lon"), None), P(None, "lat", "lon")),
        check_vma=False,
    )
```

```python
import functools
import itertools

import jax
import jax.numpy as jnp
from jax import lax
from jax.experimental import pallas as pl
from jax.experimental.pallas import tpu as pltpu
from jax.sharding import PartitionSpec as P

F32 = jnp.float32
BF16 = jnp.bfloat16
LANES = 128
EDGE = 8
HALO = 4
BACK = 2
META = 8
VMEM = pltpu.VMEM
SMEM = pltpu.SMEM


def call(body, outs, n_in, scratch=(), smem=(), flops=0, moved=0, name=None, limit=53, far=(), far_out=()):
    def spec(i, far=far, smem=smem):
        space = SMEM if i in smem else pltpu.HBM if i in far else VMEM
        return pl.BlockSpec(memory_space=space)

    specs = [spec(i) for i in range(n_in)]
    return pl.pallas_call(
        body,
        out_shape=tuple(jax.ShapeDtypeStruct(s, d) for s, d in outs),
        in_specs=specs,
        out_specs=tuple(spec(i, far_out, ()) for i in range(len(outs))),
        scratch_shapes=list(scratch),
        cost_estimate=pl.CostEstimate(flops=flops, bytes_accessed=moved, transcendentals=0),
        compiler_params=pltpu.CompilerParams(vmem_limit_bytes=limit * 2**20),
        name=name,
    )


def sigma(v):
    return 0.5 * jnp.tanh(0.5 * v) + 0.5


def dot(a, b):
    return jnp.dot(a, b, preferred_element_type=F32)


def dot_t(a, b):
    return lax.dot_general(a, b, (((1,), (1,)), ((), ())), preferred_element_type=F32)


def fetch(src, dst, sem):
    copy = pltpu.make_async_copy(src, dst, sem)
    copy.start()
    return copy


def padded(ref, src_ref):
    ref[...] = jnp.zeros_like(ref)
    ref[0 : src_ref.shape[0], :] = src_ref[...]


def edges(half, r, rows, width, first_ref, last_ref, head_ref, tail_ref):
    first_ref[r] = half[:EDGE]
    last_ref[r] = half[half.shape[0] - EDGE :]
    if r < width:
        head_ref[r] = half
    if r >= rows - width:
        tail_ref[r - rows + width] = half


def state_body(a_ref, at_ref, s_ref, first_ref, last_ref, head_ref, tail_ref):
    v, rows, cols = a_ref.shape
    pad = jnp.zeros((LANES - v, cols), F32)
    for r in range(rows):
        x = jnp.concatenate([a_ref[:, r, :], pad], axis=0).T
        at_ref[r] = x
        half = x.astype(BF16)
        s_ref[r] = half
        edges(half, r, rows, HALO, first_ref, last_ref, head_ref, tail_ref)


def sides_body(top_ref, bottom_ref, first_ref, last_ref, near_ref, far_ref):
    width, cols, _ = top_ref.shape
    rows = first_ref.shape[0]
    near_ref[0:width] = top_ref[:, :EDGE]
    near_ref[width : width + rows] = first_ref[...]
    near_ref[width + rows :] = bottom_ref[:, :EDGE]
    far_ref[0:width] = top_ref[:, cols - EDGE :]
    far_ref[width : width + rows] = last_ref[...]
    far_ref[width + rows :] = bottom_ref[:, cols - EDGE :]


def pack_body(order_ref, obs_ref, meta_ref, out_ref):
    tiles = out_ref.shape[0]
    per = out_ref.shape[1] - META

    def one(p, c):
        h = order_ref[p]
        out_ref[h, 0:per, :] = obs_ref[pl.ds(p, per, stride=tiles), :].astype(BF16)
        return c

    lax.fori_loop(0, tiles, one, 0)
    for h in range(tiles):
        out_ref[h, per : per + META, :] = meta_ref[h]


def unpack_body(order_ref, count_ref, got_ref, obs_ref, prec_ref, out_ref):
    tiles, per, _ = got_ref.shape
    prec = prec_ref[...]
    slot = lax.broadcasted_iota(jnp.int32, (per, LANES), 0) * tiles

    def one(p, c):
        h = order_ref[p]
        obs = obs_ref[pl.ds(p, per, stride=tiles), :]
        dep = (got_ref[h].astype(F32) - obs) * prec
        out_ref[pl.ds(p, per, stride=tiles), :] = jnp.where(slot + p < count_ref[0], dep, 0.0)
        return c

    lax.fori_loop(0, tiles, one, 0)


def shift_pairs(size, wrap):
    up = [(i, (i + 1) % size) for i in range(size if wrap else size - 1)]
    return up, [(j, i) for i, j in up]


def halo_rows(first, last, head, tail):
    up, down = shift_pairs(lax.axis_size("lat"), False)
    top = lax.ppermute(tail, "lat", up)
    bottom = lax.ppermute(head, "lat", down)
    shape = (first.shape[0] + 2 * head.shape[0],) + first.shape[1:]
    near, far = call(sides_body, [(shape, BF16)] * 2, 4, name="sides")(
        top, bottom, first, last
    )
    return top, bottom, near, far


def halo_columns(near, far):
    up, down = shift_pairs(lax.axis_size("lon"), True)
    left = lax.ppermute(far, "lon", up)
    right = lax.ppermute(near, "lon", down)
    return right, left


def bands(mid_ref, top_ref, bottom_ref, width):
    rows = mid_ref.shape[0]
    return (
        [(top_ref, r) for r in range(width)]
        + [(mid_ref, r) for r in range(rows)]
        + [(bottom_ref, r) for r in range(width)]
    )


def fold_row(nat_ref, e, q_n):
    slabs = [nat_ref[e, pl.ds(q, SUB, stride=q_n), :] for q in range(q_n)]
    return jnp.concatenate(slabs, axis=0)


def unfold_row(nat_ref, e, value, q_n):
    for q in range(q_n):
        nat_ref[e, pl.ds(q, SUB, stride=q_n), :] = value[q * SUB : (q + 1) * SUB]


def put_row(ref, e, value):
    n, ch = value.shape
    q_n = n // SUB
    ref[e, 1 : q_n + 1] = value.astype(BF16).reshape(q_n, SUB, ch)
    ref[e, 0] = pltpu.roll(value[n - SUB :], 1, 0).astype(BF16)
    ref[e, q_n + 1] = pltpu.roll(value[:SUB], SUB - 1, 0).astype(BF16)


def center(ref, e):
    q_n, ch = ref.shape[1] - 2, ref.shape[3]
    return ref[e, 1 : q_n + 1].reshape(q_n * SUB, ch)


def conv_rows(ref, e, count, weight):
    q_n, ch = ref.shape[1] - 2, ref.shape[3]
    parts = [
        ref[e + i : e + i + count, j : j + q_n].reshape(count * q_n * SUB, ch)
        for i in range(3)
        for j in range(3)
    ]
    return dot(jnp.concatenate(parts, axis=1), weight)


def conv_back(ref, e, count, weight_ref):
    q_n, ch = ref.shape[1] - 2, ref.shape[3]
    parts = [
        ref[e + i : e + i + count, j : j + q_n].reshape(count * q_n * SUB, ch)
        for i in range(3)
        for j in range(3)
    ]
    taps = [weight_ref[(8 - t) * ch : (9 - t) * ch, :] for t in range(9)]
    return dot_t(jnp.concatenate(parts, axis=1), jnp.concatenate(taps, axis=1))


def inside(lat_ref, a, rows, n_lat):
    g = lat_ref[0] * rows + a
    return jnp.logical_and(g >= 0, g < n_lat * rows)


STEP = 2
SUB = 16


def forward_body(
    n_lat, lat_ref, mid_ref, top_ref, bottom_ref, right_ref, left_ref, at_ref, enc_in, w_ref, ro_in,
    cols_ref, slope0_out, slope1_out,
    a0, a1, nat, back, enc_ref, ro_ref, w_v, at_v, slope0_ref, slope1_ref, sem,
):
    w0 = fetch(w_ref.at[0], w_v.at[0], sem.at[0])
    w1 = fetch(w_ref.at[1], w_v.at[1], sem.at[1])
    at_in = fetch(at_ref, at_v, sem.at[2])
    padded(enc_ref, enc_in)
    padded(ro_ref, ro_in)
    rows, cols, _ = mid_ref.shape
    q_n = a0.shape[1] - 2
    n = q_n * SUB
    for e, (src, r) in enumerate(bands(mid_ref, top_ref, bottom_ref, HALO)):
        nat[e, 0:cols, :] = src[r].astype(F32)
        nat[e, cols : cols + EDGE, :] = right_ref[e].astype(F32)
        nat[e, cols + EDGE :, :] = left_ref[e].astype(F32)
        x = fold_row(nat, e, q_n).astype(BF16)
        put_row(a0, e, dot(x, enc_ref[...]))

    def first(e):
        pre = conv_rows(a0, e, STEP, w_v[0])
        s = sigma(pre)
        act = pre * s
        slope = (s + act * (1.0 - s)).astype(BF16)
        for q in range(STEP):
            at = slice(q * n, (q + 1) * n)
            slope0_ref[e + q] = slope[at]
            h = center(a0, e + q + 1).astype(F32) + act[at]
            a = e + q - HALO + 1
            if a < 0 or a >= rows:
                h = jnp.where(inside(lat_ref, a, rows, n_lat), h, 0.0)
            put_row(a1, e + q, h)

    def second(e):
        pre = conv_rows(a1, e, STEP, w_v[1])
        s = sigma(pre)
        act = pre * s
        slope = (s + act * (1.0 - s)).astype(BF16)
        for q in range(STEP):
            at = slice(q * n, (q + 1) * n)
            slope1_ref[e + q] = slope[at]
            a = e + q - HALO + 2
            if 0 <= a < rows:
                h = center(a1, e + q + 1).astype(F32) + act[at]
                unfold_row(back, a, dot_t(h.astype(BF16), ro_ref[...]), q_n)
                cols_ref[a] = (at_v[a] + back[a, 0:cols, :]).astype(BF16)

    w0.wait()
    for e in range(0, rows + 2 * HALO - 2, STEP):
        first(e)
    out0 = fetch(slope0_ref, slope0_out, sem.at[3])
    w1.wait()
    at_in.wait()
    for e in range(0, rows + 2 * HALO - 4, STEP):
        second(e)
    out1 = fetch(slope1_ref, slope1_out, sem.at[4])
    out0.wait()
    out1.wait()


def adjoint_body(
    n_lat, lat_ref, mid_ref, top_ref, bottom_ref, right_ref, left_ref, adj_in, slope0_in, slope1_in,
    rot_in, w_in, enc_in, state_in, prior_in, prec_in,
    out_ref, b1, b0, adj2, adj1, nat, back, rot_ref, enc_ref, prec_pad,
    adj_ref, slope0_ref, slope1_ref, w_ref, state_ref, prior_ref, sem,
):
    slope1_got = fetch(slope1_in, slope1_ref, sem.at[0])
    w1 = fetch(w_in.at[1], w_ref.at[1], sem.at[1])
    slope0_got = fetch(slope0_in, slope0_ref, sem.at[2])
    w0 = fetch(w_in.at[0], w_ref.at[0], sem.at[3])
    late = [
        fetch(src, dst, sem.at[4 + i])
        for i, (src, dst) in enumerate(
            ((adj_in, adj_ref), (state_in, state_ref), (prior_in, prior_ref))
        )
    ]
    padded(rot_ref, rot_in)
    padded(enc_ref, enc_in)
    prec_pad[...] = jnp.zeros_like(prec_pad)
    prec_pad[0:1, 0 : prec_in.shape[1]] = prec_in[...]
    rows, cols, _ = mid_ref.shape
    q_n = b1.shape[1] - 2
    n = q_n * SUB
    v = out_ref.shape[0]
    prec = jnp.broadcast_to(prec_pad[0:1, :], (LANES, LANES)).T[0:v, :]
    slope1_got.wait()
    for e, (src, r) in enumerate(bands(mid_ref, top_ref, bottom_ref, BACK)):
        nat[e, 0:cols, :] = src[r].astype(F32)
        nat[e, cols : cols + EDGE, :] = right_ref[e].astype(F32)
        nat[e, cols + EDGE :, :] = left_ref[e].astype(F32)
        g = dot(fold_row(nat, e, q_n).astype(BF16), rot_ref[...])
        adj2[e] = g
        put_row(b1, e, g * slope1_ref[e].astype(F32))

    slope0_got.wait()
    w1.wait()
    for e in range(0, rows + 2, STEP):
        g = conv_back(b1, e, STEP, w_ref.at[1])
        for q in range(STEP):
            total = adj2[e + q + 1] + g[q * n : (q + 1) * n]
            adj1[e + q] = total
            h = total * slope0_ref[e + q + 2].astype(F32)
            a = e + q - 1
            if a < 0 or a >= rows:
                h = jnp.where(inside(lat_ref, a, rows, n_lat), h, 0.0)
            put_row(b0, e + q, h)

    w0.wait()
    for copy in late:
        copy.wait()
    for a in range(0, rows, STEP):
        g = conv_back(b0, a, STEP, w_ref.at[0])
        for q in range(STEP):
            total = adj1[a + q + 1] + g[q * n : (q + 1) * n]
            unfold_row(back, a + q, dot_t(total.astype(BF16), enc_ref[...]), q_n)
            grow = back[a + q, 0:cols, :] + adj_ref[a + q]
            diff = state_ref[:, a + q, :] - prior_ref[:, a + q, :]
            out_ref[:, a + q, :] = prec * diff + grow.T[0:v, :]


BLOCK = 1024


def observe_body(
    table_ref, cols_ref, got_in, win_ref, wout_ref, prec_ref,
    adj_ref, half_ref, first_ref, last_ref, head_ref, tail_ref, pred_ref,
    xs, slope, grid, hot, weights, fa, meta, got_ref, sem,
):
    got = fetch(got_in, got_ref, sem.at[0])
    rows, cols, _ = cols_ref.shape
    cells = rows * cols
    half = cells // 2
    tiles, per, nch = pred_ref.shape
    obs_n = tiles * per
    group = LANES // per
    prec2 = prec_ref[...] * prec_ref[...]
    c0 = cols_ref[...].reshape(cells, LANES)
    c1 = pltpu.roll(c0.astype(F32), cells - 1, 0).astype(BF16)
    xs[0] = c0
    xs[1] = c1
    xs[2] = jnp.concatenate([c0[cols:], c0[:cols]], axis=0)
    xs[3] = jnp.concatenate([c1[cols:], c1[:cols]], axis=0)
    rest = jnp.zeros((1, LANES), F32)
    got.wait()
    for m in range(obs_n // LANES):
        total = got_ref[m * group, per : per + META, :].astype(F32)
        for g in range(1, group):
            total += got_ref[m * group + g, per : per + META, :].astype(F32)
        meta[m] = total
        rest += jnp.where(total[2:3] == table_ref[0, 4].astype(F32), 0.0, 1.0)
    trips = jnp.where(jnp.sum(rest) > 0.0, table_ref.shape[0], 1)
    fa[...] = jnp.zeros_like(fa)

    def arrangement(cls, carry):
        place = [table_ref[cls, f] for f in range(4)]
        code = table_ref[cls, 4].astype(F32)

        def forward(k, c):
            at = pl.ds(k * BLOCK, BLOCK)
            x = jnp.concatenate([xs[place[f], at, :] for f in range(4)], axis=1)
            inner = dot(x, win_ref[...])
            s = sigma(inner)
            act = inner * s
            slope[at, :] = (s + act * (1.0 - s)).astype(BF16)
            grid[at, :] = dot(act.astype(BF16), wout_ref[...]).astype(BF16)
            return c

        lax.fori_loop(0, cells // BLOCK, forward, 0)
        both = jnp.concatenate([grid[0:half, :], grid[half:, :]], axis=1)
        lane = lax.broadcasted_iota(jnp.int32, (LANES, LANES), 1).astype(F32)
        sub = lax.broadcasted_iota(jnp.int32, (LANES, LANES), 0).astype(F32)
        top = float(rows // 2)

        def gather(m, c):
            mine = meta[m, 2:3, :] == code
            row = jnp.broadcast_to(jnp.where(mine, meta[m, 0:1, :], float(rows)), (LANES, LANES))
            col = jnp.broadcast_to(meta[m, 1:2, :], (LANES, LANES))
            row_t, col_t = row.T, col.T
            local = jnp.where(row_t < top, row_t, row_t - top)
            value = jnp.where(col_t == lane, local, -1.0)
            sel = jnp.concatenate(
                [jnp.where(value == float(t), 1.0, 0.0).astype(BF16) for t in range(rows // 2)],
                axis=1,
            )
            out = dot(sel, both)
            upper = row_t >= top
            pred = jnp.where(upper, out[:, nch:], out[:, :nch])
            pred = jnp.where(row_t < float(rows), pred, 0.0)
            obs = got_ref[pl.ds(m * group, group), 0:per, :].astype(F32).reshape(LANES, nch)
            w = (pred - obs) * prec2
            at = pl.ds(m * LANES, LANES)
            weights[at, 0:nch] = jnp.where(upper, 0.0, w).astype(BF16)
            weights[at, nch:] = jnp.where(upper, w, 0.0).astype(BF16)
            pred = pred.reshape(group, per, nch)
            where = pl.ds(m * group, group)

            @pl.when(cls == 0)
            def _():
                pred_ref[where] = pred.astype(BF16)

            @pl.when(cls > 0)
            def _():
                pred_ref[where] = (pred_ref[where].astype(F32) + pred).astype(BF16)

            local = jnp.where(row < top, row, row - top)
            value = jnp.where(col == sub, local, -1.0)
            for t in range(rows // 2):
                hot[t * LANES : (t + 1) * LANES, pl.ds(pl.multiple_of(m * LANES, LANES), LANES)] = (
                    jnp.where(value == float(t), 1.0, 0.0).astype(BF16)
                )
            return c

        lax.fori_loop(0, obs_n // LANES, gather, 0)

        def scatter(k, c):
            at = pl.ds(k * BLOCK, BLOCK)
            total = dot(hot[at, :], weights[...])
            grid[at, :] = total[:, :nch].astype(BF16)
            grid[pl.ds(half + k * BLOCK, BLOCK), :] = total[:, nch:].astype(BF16)
            return c

        lax.fori_loop(0, half // BLOCK, scatter, 0)

        def backward(k, c):
            at = pl.ds(k * BLOCK, BLOCK)
            act = dot_t(grid[at, :], wout_ref[...])
            inner = (act * slope[at, :].astype(F32)).astype(BF16)
            x = dot_t(inner, win_ref[...])
            for f in range(4):
                fa[place[f], at, :] += x[:, f * LANES : (f + 1) * LANES]
            return c

        lax.fori_loop(0, cells // BLOCK, backward, 0)
        return carry

    lax.fori_loop(0, trips, arrangement, 0)
    high = fa[3]
    one = fa[1] + jnp.concatenate([high[cells - cols :], high[: cells - cols]], axis=0)
    low = fa[2]
    total = fa[0] + jnp.concatenate([low[cells - cols :], low[: cells - cols]], axis=0)
    total += pltpu.roll(one, 1, 0)
    total = total.reshape(rows, cols, LANES)
    adj_ref[...] = total
    total = total.astype(BF16)
    half_ref[...] = total
    for r in range(rows):
        edges(total[r], r, rows, BACK, first_ref, last_ref, head_ref, tail_ref)


def arrangement_table():
    orders = list(itertools.permutations(range(4)))
    first = (0, 2, 1, 3)
    orders.remove(first)
    return [
        list(o) + [sum(q * 4**f for f, q in enumerate(o))] for o in [first] + orders
    ]


def on_device(
    analysis_vector,
    prior_estimate,
    prior_precision,
    encoder_weight,
    conv_weights,
    readout_matrix,
    obs_in_weight,
    obs_out_weight,
    obs_values,
    obs_precision,
    foot_cells,
    obs_count,
):
    v, rows, cols = analysis_vector.shape
    n_lat, n_lon = lax.axis_size("lat"), lax.axis_size("lon")
    tiles = n_lat * n_lon
    obs_n, foot = foot_cells.shape
    per = obs_n // tiles
    ch = encoder_weight.shape[1]
    hid, nch = obs_out_weight.shape
    width = cols + 2 * EDGE
    cells = rows * cols
    lat, lon = lax.axis_index("lat"), lax.axis_index("lon")
    lat_id = lat.reshape(1)

    strip = (rows, EDGE, LANES)
    at, s16, *rim = call(
        state_body,
        [((rows, cols, LANES), F32), ((rows, cols, LANES), BF16)]
        + [(strip, BF16)] * 2 + [((HALO, cols, LANES), BF16)] * 2,
        1, moved=cells * v * 8, name="state",
    )(analysis_vector)
    foot_cells, obs_sent, *rim = lax.optimization_barrier((foot_cells, obs_values, *rim))
    top, bottom, near, far = halo_rows(*rim)

    lon_total = cols * n_lon
    lat_g, lon_g = foot_cells // lon_total, foot_cells % lon_total
    order = lat_g[:tiles, 0] // rows * n_lon + lon_g[:tiles, 0] // cols
    base_lat, base_lon = jnp.min(lat_g, axis=1), jnp.min(lon_g, axis=1)
    place = (lat_g - base_lat[:, None]) * 2 + (lon_g - base_lon[:, None])
    code = jnp.sum(place * (4 ** jnp.arange(foot)), axis=1)
    valid = jnp.arange(obs_n) < obs_count[0]
    local = jnp.where(valid, base_lat % rows, rows)
    fields = jnp.stack([local, base_lon % cols, code]).astype(BF16).reshape(3, per, tiles)
    pick = (order[None, :] == jnp.arange(tiles)[:, None]).astype(BF16)
    meta = jnp.einsum("fkp,hp->hfk", fields, pick, preferred_element_type=F32).astype(BF16)
    group = LANES // per
    mine = jnp.arange(group) == (lat * n_lon + lon) % group
    meta = jnp.where(mine[:, None], meta[:, :, None, :], jnp.zeros((), BF16)).reshape(tiles, 3, LANES)
    meta = jnp.pad(meta, ((0, 0), (0, META - 3), (0, 0)))
    (send,) = call(
        pack_body, [((tiles, per + META, nch), BF16)], 3, smem=(0,), moved=obs_n * nch * 6, name="pack"
    )(order, obs_sent, meta)
    send, near, far = lax.optimization_barrier((send, near, far))
    right, left = halo_columns(near, far)
    got = lax.all_to_all(send, ("lat", "lon"), split_axis=0, concat_axis=0, tiled=True)

    rot = readout_matrix.T
    win = jnp.pad(obs_in_weight, ((0, 0), (0, LANES - v), (0, 0))).reshape(foot * LANES, hid)
    w_fwd = conv_weights.reshape(conv_weights.shape[0], 9 * ch, ch)

    conv_flops = 2 * cells * 9 * ch * ch
    cols16, slope0, slope1 = call(
        functools.partial(forward_body, n_lat),
        [
            ((rows, cols, LANES), BF16),
            ((rows + 2 * HALO - 2, width, ch), BF16),
            ((rows + 2 * HALO - 4, width, ch), BF16),
        ],
        10,
        [
            VMEM((rows + 2 * HALO, width // SUB + 2, SUB, ch), BF16),
            VMEM((rows + 2 * HALO - 2, width // SUB + 2, SUB, ch), BF16),
            VMEM((rows + 2 * HALO, width, LANES), F32),
            VMEM((rows, width, LANES), F32),
            VMEM((LANES, ch), BF16),
            VMEM((LANES, ch), BF16),
            VMEM(w_fwd.shape, BF16),
            VMEM((rows, cols, LANES), F32),
            VMEM((rows + 2 * HALO - 2, width, ch), BF16),
            VMEM((rows + 2 * HALO - 4, width, ch), BF16),
            pltpu.SemaphoreType.DMA((5,)),
        ],
        (0,), 3 * conv_flops, cells * ch * 8, "forward", far=(6, 8), far_out=(1, 2),
    )(lat_id, s16, top, bottom, right, left, at, encoder_weight, w_fwd, rot)

    adj, adj16, *rim, pred = call(
        observe_body,
        [((rows, cols, LANES), F32), ((rows, cols, LANES), BF16)]
        + [(strip, BF16)] * 2 + [((BACK, cols, LANES), BF16)] * 2 + [((tiles, per, nch), BF16)],
        6,
        [
            VMEM((4, cells, LANES), BF16),
            VMEM((cells, hid), BF16),
            VMEM((cells, nch), BF16),
            VMEM((cells // 2, obs_n), BF16),
            VMEM((obs_n, 2 * nch), BF16),
            VMEM((4, cells, LANES), F32),
            VMEM((obs_n // LANES, META, LANES), F32),
            VMEM(got.shape, BF16),
            pltpu.SemaphoreType.DMA((1,)),
        ],
        (0,), 4 * cells * hid * (foot * LANES + nch), cells * hid * 4, "observe", far=(2,),
    )(
        jnp.array(arrangement_table(), jnp.int32), cols16, got, win, obs_out_weight,
        obs_precision[None, :],
    )
    back = lax.all_to_all(pred, ("lat", "lon"), split_axis=0, concat_axis=0, tiled=True)

    top, bottom, near, far = halo_rows(*rim)
    right, left = halo_columns(near, far)
    (derivative,) = call(
        functools.partial(adjoint_body, n_lat),
        [((v, rows, cols), F32)],
        15,
        [
            VMEM((rows + 2 * BACK, width // SUB + 2, SUB, ch), BF16),
            VMEM((rows + 2, width // SUB + 2, SUB, ch), BF16),
            VMEM((rows + 2 * BACK, width, ch), F32),
            VMEM((rows + 2, width, ch), F32),
            VMEM((rows + 2 * BACK, width, LANES), F32),
            VMEM((rows, width, LANES), F32),
            VMEM((LANES, ch), BF16),
            VMEM((LANES, ch), BF16),
            VMEM((8, LANES), F32),
            VMEM((rows, cols, LANES), F32),
            VMEM(slope0.shape, BF16),
            VMEM(slope1.shape, BF16),
            VMEM(w_fwd.shape, BF16),
            VMEM((v, rows, cols), F32),
            VMEM((v, rows, cols), F32),
            pltpu.SemaphoreType.DMA((7,)),
        ],
        (0,), 3 * conv_flops, cells * ch * 8, "adjoint", far=(6, 7, 8, 10, 12, 13),
    )(
        lat_id, adj16, top, bottom, right, left, adj, slope0, slope1, rot, w_fwd, encoder_weight,
        analysis_vector, prior_estimate, prior_precision[None, :],
    )
    (departures,) = call(
        unpack_body, [((obs_n, nch), F32)], 5, smem=(0, 1), moved=obs_n * nch * 10, name="unpack"
    )(order, obs_count, back, obs_values, obs_precision[None, :])
    return departures, derivative


def solution(mesh):
    return jax.shard_map(
        on_device,
        mesh=mesh,
        in_specs=(
            P(None, "lat", "lon"),
            P(None, "lat", "lon"),
            P(),
            P(),
            P(),
            P(),
            P(),
            P(),
            P(("lat", "lon"), None),
            P(),
            P(("lat", "lon"), None),
            P(("lat", "lon")),
        ),
        out_specs=(P(("lat", "lon"), None), P(None, "lat", "lon")),
        check_vma=False,
    )
```

```python
import functools
import itertools

import jax
import jax.numpy as jnp
from jax import lax
from jax.experimental import pallas as pl
from jax.experimental.pallas import tpu as pltpu
from jax.sharding import PartitionSpec as P


F32 = jnp.float32
BF16 = jnp.bfloat16
LANES = 128
EDGE = 8
HALO = 4
BACK = 2
META = 8
VMEM = pltpu.VMEM
SMEM = pltpu.SMEM


def call(body, outs, n_in, scratch=(), smem=(), flops=0, moved=0, limit=53, far=(), far_out=()):
    def spec(i, far=far, smem=smem):
        space = SMEM if i in smem else pltpu.HBM if i in far else VMEM
        return pl.BlockSpec(memory_space=space)

    specs = [spec(i) for i in range(n_in)]
    return pl.pallas_call(
        body,
        out_shape=tuple(jax.ShapeDtypeStruct(s, d) for s, d in outs),
        in_specs=specs,
        out_specs=tuple(spec(i, far_out, ()) for i in range(len(outs))),
        scratch_shapes=list(scratch),
        cost_estimate=pl.CostEstimate(flops=flops, bytes_accessed=moved, transcendentals=0),
        compiler_params=pltpu.CompilerParams(vmem_limit_bytes=limit * 2**20),
    )


def sigma(v):
    return 0.5 * jnp.tanh(0.5 * v) + 0.5


def dot(a, b):
    return jnp.dot(a, b, preferred_element_type=F32)


def dot_t(a, b):
    return lax.dot_general(a, b, (((1,), (1,)), ((), ())), preferred_element_type=F32)


def fetch(src, dst, sem):
    copy = pltpu.make_async_copy(src, dst, sem)
    copy.start()
    return copy


def padded(ref, src_ref):
    ref[...] = jnp.zeros_like(ref)
    ref[0 : src_ref.shape[0], :] = src_ref[...]


def edges(half, r, rows, width, first_ref, last_ref, head_ref, tail_ref):
    first_ref[r] = half[:EDGE]
    last_ref[r] = half[half.shape[0] - EDGE :]
    if r < width:
        head_ref[r] = half
    if r >= rows - width:
        tail_ref[r - rows + width] = half


def state_body(a_ref, at_ref, s_ref, first_ref, last_ref, head_ref, tail_ref):
    v, rows, cols = a_ref.shape
    pad = jnp.zeros((LANES - v, cols), F32)
    for r in range(rows):
        x = jnp.concatenate([a_ref[:, r, :], pad], axis=0).T
        at_ref[r] = x
        half = x.astype(BF16)
        s_ref[r] = half
        edges(half, r, rows, HALO, first_ref, last_ref, head_ref, tail_ref)


def sides_body(top_ref, bottom_ref, first_ref, last_ref, near_ref, far_ref):
    width, cols, _ = top_ref.shape
    rows = first_ref.shape[0]
    near_ref[0:width] = top_ref[:, :EDGE]
    near_ref[width : width + rows] = first_ref[...]
    near_ref[width + rows :] = bottom_ref[:, :EDGE]
    far_ref[0:width] = top_ref[:, cols - EDGE :]
    far_ref[width : width + rows] = last_ref[...]
    far_ref[width + rows :] = bottom_ref[:, cols - EDGE :]


def pack_body(order_ref, obs_ref, meta_ref, out_ref):
    tiles = out_ref.shape[0]
    per = out_ref.shape[1] - META

    def one(p, c):
        h = order_ref[p]
        out_ref[h, 0:per, :] = obs_ref[pl.ds(p, per, stride=tiles), :].astype(BF16)
        return c

    lax.fori_loop(0, tiles, one, 0, unroll=8)
    for h in range(tiles):
        out_ref[h, per : per + META, :] = meta_ref[h]


def unpack_body(order_ref, count_ref, got_ref, obs_ref, prec_ref, out_ref):
    tiles, per, _ = got_ref.shape
    prec = prec_ref[...]
    slot = lax.broadcasted_iota(jnp.int32, (per, LANES), 0) * tiles

    def one(p, c):
        h = order_ref[p]
        obs = obs_ref[pl.ds(p, per, stride=tiles), :]
        dep = (got_ref[h].astype(F32) - obs) * prec
        out_ref[pl.ds(p, per, stride=tiles), :] = jnp.where(slot + p < count_ref[0], dep, 0.0)
        return c

    lax.fori_loop(0, tiles, one, 0, unroll=8)


def shift_pairs(size, wrap):
    up = [(i, (i + 1) % size) for i in range(size if wrap else size - 1)]
    return up, [(j, i) for i, j in up]


def halo_rows(first, last, head, tail):
    up, down = shift_pairs(lax.axis_size("lat"), False)
    top = lax.ppermute(tail, "lat", up)
    bottom = lax.ppermute(head, "lat", down)
    shape = (first.shape[0] + 2 * head.shape[0],) + first.shape[1:]
    near, far = call(sides_body, [(shape, BF16)] * 2, 4)(
        top, bottom, first, last
    )
    return top, bottom, near, far


def halo_columns(near, far):
    up, down = shift_pairs(lax.axis_size("lon"), True)
    left = lax.ppermute(far, "lon", up)
    right = lax.ppermute(near, "lon", down)
    return right, left


def bands(mid_ref, top_ref, bottom_ref, width):
    rows = mid_ref.shape[0]
    return (
        [(top_ref, r) for r in range(width)]
        + [(mid_ref, r) for r in range(rows)]
        + [(bottom_ref, r) for r in range(width)]
    )


def fold_row(nat_ref, e, q_n):
    slabs = [nat_ref[e, pl.ds(q, SUB, stride=q_n), :] for q in range(q_n)]
    return jnp.concatenate(slabs, axis=0)


def unfold_row(nat_ref, e, value, q_n):
    for q in range(q_n):
        nat_ref[e, pl.ds(q, SUB, stride=q_n), :] = value[q * SUB : (q + 1) * SUB]


def put_row(ref, e, value):
    n, ch = value.shape
    q_n = n // SUB
    ref[e, 1 : q_n + 1] = value.astype(BF16).reshape(q_n, SUB, ch)
    ref[e, 0] = pltpu.roll(value[n - SUB :], 1, 0).astype(BF16)
    ref[e, q_n + 1] = pltpu.roll(value[:SUB], SUB - 1, 0).astype(BF16)


def center(ref, e):
    q_n, ch = ref.shape[1] - 2, ref.shape[3]
    return ref[e, 1 : q_n + 1].reshape(q_n * SUB, ch)


def conv_rows(ref, e, count, weight):
    q_n, ch = ref.shape[1] - 2, ref.shape[3]
    parts = [
        ref[e + i : e + i + count, j : j + q_n].reshape(count * q_n * SUB, ch)
        for i in range(3)
        for j in range(3)
    ]
    return dot(jnp.concatenate(parts, axis=1), weight)


def conv_back(ref, e, count, weight_ref):
    q_n, ch = ref.shape[1] - 2, ref.shape[3]
    parts = [
        ref[e + i : e + i + count, j : j + q_n].reshape(count * q_n * SUB, ch)
        for i in range(3)
        for j in range(3)
    ]
    taps = [weight_ref[(8 - t) * ch : (9 - t) * ch, :] for t in range(9)]
    return dot_t(jnp.concatenate(parts, axis=1), jnp.concatenate(taps, axis=1))


def inside(lat_ref, a, rows, n_lat):
    g = lat_ref[0] * rows + a
    return jnp.logical_and(g >= 0, g < n_lat * rows)


STEP = 2
SUB = 16


def forward_body(
    n_lat, lat_ref, mid_ref, top_ref, bottom_ref, right_ref, left_ref, at_ref, enc_in, w_ref, ro_in,
    cols_ref, slope0_out, slope1_out,
    a0, a1, nat, back, enc_ref, ro_ref, w_v, at_v, slope0_ref, slope1_ref, sem,
):
    w0 = fetch(w_ref.at[0], w_v.at[0], sem.at[0])
    w1 = fetch(w_ref.at[1], w_v.at[1], sem.at[1])
    at_in = fetch(at_ref, at_v, sem.at[2])
    padded(enc_ref, enc_in)
    padded(ro_ref, ro_in)
    rows, cols, _ = mid_ref.shape
    q_n = a0.shape[1] - 2
    n = q_n * SUB
    for e, (src, r) in enumerate(bands(mid_ref, top_ref, bottom_ref, HALO)):
        nat[e, 0:cols, :] = src[r].astype(F32)
        nat[e, cols : cols + EDGE, :] = right_ref[e].astype(F32)
        nat[e, cols + EDGE :, :] = left_ref[e].astype(F32)
        x = fold_row(nat, e, q_n).astype(BF16)
        put_row(a0, e, dot(x, enc_ref[...]))

    def first(e):
        pre = conv_rows(a0, e, STEP, w_v[0])
        s = sigma(pre)
        act = pre * s
        slope = (s + act * (1.0 - s)).astype(BF16)
        for q in range(STEP):
            at = slice(q * n, (q + 1) * n)
            slope0_ref[e + q] = slope[at]
            h = center(a0, e + q + 1).astype(F32) + act[at]
            a = e + q - HALO + 1
            if a < 0 or a >= rows:
                h = jnp.where(inside(lat_ref, a, rows, n_lat), h, 0.0)
            put_row(a1, e + q, h)

    def second(e):
        pre = conv_rows(a1, e, STEP, w_v[1])
        s = sigma(pre)
        act = pre * s
        slope = (s + act * (1.0 - s)).astype(BF16)
        for q in range(STEP):
            at = slice(q * n, (q + 1) * n)
            slope1_ref[e + q] = slope[at]
            a = e + q - HALO + 2
            if 0 <= a < rows:
                h = center(a1, e + q + 1).astype(F32) + act[at]
                unfold_row(back, a, dot_t(h.astype(BF16), ro_ref[...]), q_n)
                cols_ref[a] = (at_v[a] + back[a, 0:cols, :]).astype(BF16)

    w0.wait()
    for e in range(0, rows + 2 * HALO - 2, STEP):
        first(e)
    out0 = fetch(slope0_ref, slope0_out, sem.at[3])
    w1.wait()
    at_in.wait()
    for e in range(0, rows + 2 * HALO - 4, STEP):
        second(e)
    out1 = fetch(slope1_ref, slope1_out, sem.at[4])
    out0.wait()
    out1.wait()


def adjoint_body(
    n_lat, lat_ref, mid_ref, top_ref, bottom_ref, right_ref, left_ref, adj_in, slope0_in, slope1_in,
    rot_in, w_in, enc_in, state_in, prior_in, prec_in,
    out_ref, b1, b0, adj2, adj1, nat, back, rot_ref, enc_ref, prec_pad,
    adj_ref, slope0_ref, slope1_ref, w_ref, state_ref, prior_ref, sem,
):
    slope1_got = fetch(slope1_in, slope1_ref, sem.at[0])
    w1 = fetch(w_in.at[1], w_ref.at[1], sem.at[1])
    slope0_got = fetch(slope0_in, slope0_ref, sem.at[2])
    w0 = fetch(w_in.at[0], w_ref.at[0], sem.at[3])
    late = [
        fetch(src, dst, sem.at[4 + i])
        for i, (src, dst) in enumerate(
            ((adj_in, adj_ref), (state_in, state_ref), (prior_in, prior_ref))
        )
    ]
    padded(rot_ref, rot_in)
    padded(enc_ref, enc_in)
    prec_pad[...] = jnp.zeros_like(prec_pad)
    prec_pad[0:1, 0 : prec_in.shape[1]] = prec_in[...]
    rows, cols, _ = mid_ref.shape
    q_n = b1.shape[1] - 2
    n = q_n * SUB
    v = out_ref.shape[0]
    prec = jnp.broadcast_to(prec_pad[0:1, :], (LANES, LANES)).T[0:v, :]
    slope1_got.wait()
    for e, (src, r) in enumerate(bands(mid_ref, top_ref, bottom_ref, BACK)):
        nat[e, 0:cols, :] = src[r].astype(F32)
        nat[e, cols : cols + EDGE, :] = right_ref[e].astype(F32)
        nat[e, cols + EDGE :, :] = left_ref[e].astype(F32)
        g = dot(fold_row(nat, e, q_n).astype(BF16), rot_ref[...])
        adj2[e] = g
        put_row(b1, e, g * slope1_ref[e].astype(F32))

    slope0_got.wait()
    w1.wait()
    for e in range(0, rows + 2, STEP):
        g = conv_back(b1, e, STEP, w_ref.at[1])
        for q in range(STEP):
            total = adj2[e + q + 1] + g[q * n : (q + 1) * n]
            adj1[e + q] = total
            h = total * slope0_ref[e + q + 2].astype(F32)
            a = e + q - 1
            if a < 0 or a >= rows:
                h = jnp.where(inside(lat_ref, a, rows, n_lat), h, 0.0)
            put_row(b0, e + q, h)

    w0.wait()
    for copy in late:
        copy.wait()
    for a in range(0, rows, STEP):
        g = conv_back(b0, a, STEP, w_ref.at[0])
        for q in range(STEP):
            total = adj1[a + q + 1] + g[q * n : (q + 1) * n]
            unfold_row(back, a + q, dot_t(total.astype(BF16), enc_ref[...]), q_n)
            grow = back[a + q, 0:cols, :] + adj_ref[a + q]
            diff = state_ref[:, a + q, :] - prior_ref[:, a + q, :]
            out_ref[:, a + q, :] = prec * diff + grow.T[0:v, :]


BLOCK = 1024


def observe_body(
    table_ref, cols_ref, got_in, win_ref, wout_ref, prec_ref,
    adj_ref, half_ref, first_ref, last_ref, head_ref, tail_ref, pred_ref,
    xs, slope, grid, hot, weights, fa, meta, got_ref, sem,
):
    got = fetch(got_in, got_ref, sem.at[0])
    rows, cols, _ = cols_ref.shape
    cells = rows * cols
    half = cells // 2
    tiles, per, nch = pred_ref.shape
    obs_n = tiles * per
    group = LANES // per
    prec2 = prec_ref[...] * prec_ref[...]
    c0 = cols_ref[...].reshape(cells, LANES)
    c1 = pltpu.roll(c0.astype(F32), cells - 1, 0).astype(BF16)
    xs[0] = c0
    xs[1] = c1
    xs[2] = jnp.concatenate([c0[cols:], c0[:cols]], axis=0)
    xs[3] = jnp.concatenate([c1[cols:], c1[:cols]], axis=0)
    rest = jnp.zeros((1, LANES), F32)
    got.wait()
    for m in range(obs_n // LANES):
        total = got_ref[m * group, per : per + META, :].astype(F32)
        for g in range(1, group):
            total += got_ref[m * group + g, per : per + META, :].astype(F32)
        meta[m] = total
        rest += jnp.where(total[2:3] == table_ref[0, 4].astype(F32), 0.0, 1.0)
    trips = jnp.where(jnp.sum(rest) > 0.0, table_ref.shape[0], 1)
    fa[...] = jnp.zeros_like(fa)

    def arrangement(cls, carry):
        place = [table_ref[cls, f] for f in range(4)]
        code = table_ref[cls, 4].astype(F32)

        def forward(k, c):
            at = pl.ds(k * BLOCK, BLOCK)
            x = jnp.concatenate([xs[place[f], at, :] for f in range(4)], axis=1)
            inner = dot(x, win_ref[...])
            s = sigma(inner)
            act = inner * s
            slope[at, :] = (s + act * (1.0 - s)).astype(BF16)
            grid[at, :] = dot(act.astype(BF16), wout_ref[...]).astype(BF16)
            return c

        lax.fori_loop(0, cells // BLOCK, forward, 0)
        both = jnp.concatenate([grid[0:half, :], grid[half:, :]], axis=1)
        lane = lax.broadcasted_iota(jnp.int32, (LANES, LANES), 1).astype(F32)
        sub = lax.broadcasted_iota(jnp.int32, (LANES, LANES), 0).astype(F32)
        top = float(rows // 2)

        def gather(m, c):
            mine = meta[m, 2:3, :] == code
            row = jnp.broadcast_to(jnp.where(mine, meta[m, 0:1, :], float(rows)), (LANES, LANES))
            col = jnp.broadcast_to(meta[m, 1:2, :], (LANES, LANES))
            row_t, col_t = row.T, col.T
            local = jnp.where(row_t < top, row_t, row_t - top)
            value = jnp.where(col_t == lane, local, -1.0)
            sel = jnp.concatenate(
                [jnp.where(value == float(t), 1.0, 0.0).astype(BF16) for t in range(rows // 2)],
                axis=1,
            )
            out = dot(sel, both)
            upper = row_t >= top
            pred = jnp.where(upper, out[:, nch:], out[:, :nch])
            pred = jnp.where(row_t < float(rows), pred, 0.0)
            obs = got_ref[pl.ds(m * group, group), 0:per, :].astype(F32).reshape(LANES, nch)
            w = (pred - obs) * prec2
            at = pl.ds(m * LANES, LANES)
            weights[at, 0:nch] = jnp.where(upper, 0.0, w).astype(BF16)
            weights[at, nch:] = jnp.where(upper, w, 0.0).astype(BF16)
            pred = pred.reshape(group, per, nch)
            where = pl.ds(m * group, group)

            @pl.when(cls == 0)
            def _():
                pred_ref[where] = pred.astype(BF16)

            @pl.when(cls > 0)
            def _():
                pred_ref[where] = (pred_ref[where].astype(F32) + pred).astype(BF16)

            local = jnp.where(row < top, row, row - top)
            value = jnp.where(col == sub, local, -1.0)
            for t in range(rows // 2):
                hot[t * LANES : (t + 1) * LANES, pl.ds(pl.multiple_of(m * LANES, LANES), LANES)] = (
                    jnp.where(value == float(t), 1.0, 0.0).astype(BF16)
                )
            return c

        lax.fori_loop(0, obs_n // LANES, gather, 0)

        def scatter(k, c):
            at = pl.ds(k * BLOCK, BLOCK)
            total = dot(hot[at, :], weights[...])
            grid[at, :] = total[:, :nch].astype(BF16)
            grid[pl.ds(half + k * BLOCK, BLOCK), :] = total[:, nch:].astype(BF16)
            return c

        lax.fori_loop(0, half // BLOCK, scatter, 0)

        def backward(k, c):
            at = pl.ds(k * BLOCK, BLOCK)
            act = dot_t(grid[at, :], wout_ref[...])
            inner = (act * slope[at, :].astype(F32)).astype(BF16)
            x = dot_t(inner, win_ref[...])
            for f in range(4):
                fa[place[f], at, :] += x[:, f * LANES : (f + 1) * LANES]
            return c

        lax.fori_loop(0, cells // BLOCK, backward, 0)
        return carry

    lax.fori_loop(0, trips, arrangement, 0)
    high = fa[3]
    one = fa[1] + jnp.concatenate([high[cells - cols :], high[: cells - cols]], axis=0)
    low = fa[2]
    total = fa[0] + jnp.concatenate([low[cells - cols :], low[: cells - cols]], axis=0)
    total += pltpu.roll(one, 1, 0)
    total = total.reshape(rows, cols, LANES)
    adj_ref[...] = total
    total = total.astype(BF16)
    half_ref[...] = total
    for r in range(rows):
        edges(total[r], r, rows, BACK, first_ref, last_ref, head_ref, tail_ref)


def arrangement_table():
    orders = list(itertools.permutations(range(4)))
    first = (0, 2, 1, 3)
    orders.remove(first)
    return [
        list(o) + [sum(q * 4**f for f, q in enumerate(o))] for o in [first] + orders
    ]


def on_device(
    analysis_vector,
    prior_estimate,
    prior_precision,
    encoder_weight,
    conv_weights,
    readout_matrix,
    obs_in_weight,
    obs_out_weight,
    obs_values,
    obs_precision,
    foot_cells,
    obs_count,
):
    v, rows, cols = analysis_vector.shape
    n_lat, n_lon = lax.axis_size("lat"), lax.axis_size("lon")
    tiles = n_lat * n_lon
    obs_n, foot = foot_cells.shape
    per = obs_n // tiles
    ch = encoder_weight.shape[1]
    hid, nch = obs_out_weight.shape
    width = cols + 2 * EDGE
    cells = rows * cols
    lat, lon = lax.axis_index("lat"), lax.axis_index("lon")
    lat_id = lat.reshape(1)

    strip = (rows, EDGE, LANES)
    at, s16, *rim = call(
        state_body,
        [((rows, cols, LANES), F32), ((rows, cols, LANES), BF16)]
        + [(strip, BF16)] * 2 + [((HALO, cols, LANES), BF16)] * 2,
        1, moved=cells * v * 8,
    )(analysis_vector)
    foot_cells, obs_sent, *rim = lax.optimization_barrier((foot_cells, obs_values, *rim))
    top, bottom, near, far = halo_rows(*rim)

    lon_total = cols * n_lon
    lat_g, lon_g = foot_cells // lon_total, foot_cells % lon_total
    order = lat_g[:tiles, 0] // rows * n_lon + lon_g[:tiles, 0] // cols
    base_lat, base_lon = jnp.min(lat_g, axis=1), jnp.min(lon_g, axis=1)
    place = (lat_g - base_lat[:, None]) * 2 + (lon_g - base_lon[:, None])
    code = jnp.sum(place * (4 ** jnp.arange(foot)), axis=1)
    valid = jnp.arange(obs_n) < obs_count[0]
    local = jnp.where(valid, base_lat % rows, rows)
    fields = jnp.stack([local, base_lon % cols, code]).astype(BF16).reshape(3, per, tiles)
    pick = (order[None, :] == jnp.arange(tiles)[:, None]).astype(BF16)
    meta = jnp.einsum("fkp,hp->hfk", fields, pick, preferred_element_type=F32).astype(BF16)
    group = LANES // per
    mine = jnp.arange(group) == (lat * n_lon + lon) % group
    meta = jnp.where(mine[:, None], meta[:, :, None, :], jnp.zeros((), BF16)).reshape(tiles, 3, LANES)
    meta = jnp.pad(meta, ((0, 0), (0, META - 3), (0, 0)))
    (send,) = call(
        pack_body, [((tiles, per + META, nch), BF16)], 3, smem=(0,), moved=obs_n * nch * 6
    )(order, obs_sent, meta)
    send, near, far = lax.optimization_barrier((send, near, far))
    right, left = halo_columns(near, far)
    got = lax.all_to_all(send, ("lat", "lon"), split_axis=0, concat_axis=0, tiled=True)

    rot = readout_matrix.T
    win = jnp.pad(obs_in_weight, ((0, 0), (0, LANES - v), (0, 0))).reshape(foot * LANES, hid)
    w_fwd = conv_weights.reshape(conv_weights.shape[0], 9 * ch, ch)

    conv_flops = 2 * cells * 9 * ch * ch
    cols16, slope0, slope1 = call(
        functools.partial(forward_body, n_lat),
        [
            ((rows, cols, LANES), BF16),
            ((rows + 2 * HALO - 2, width, ch), BF16),
            ((rows + 2 * HALO - 4, width, ch), BF16),
        ],
        10,
        [
            VMEM((rows + 2 * HALO, width // SUB + 2, SUB, ch), BF16),
            VMEM((rows + 2 * HALO - 2, width // SUB + 2, SUB, ch), BF16),
            VMEM((rows + 2 * HALO, width, LANES), F32),
            VMEM((rows, width, LANES), F32),
            VMEM((LANES, ch), BF16),
            VMEM((LANES, ch), BF16),
            VMEM(w_fwd.shape, BF16),
            VMEM((rows, cols, LANES), F32),
            VMEM((rows + 2 * HALO - 2, width, ch), BF16),
            VMEM((rows + 2 * HALO - 4, width, ch), BF16),
            pltpu.SemaphoreType.DMA((5,)),
        ],
        (0,), 3 * conv_flops, cells * ch * 8, far=(6, 8), far_out=(1, 2),
    )(lat_id, s16, top, bottom, right, left, at, encoder_weight, w_fwd, rot)

    adj, adj16, *rim, pred = call(
        observe_body,
        [((rows, cols, LANES), F32), ((rows, cols, LANES), BF16)]
        + [(strip, BF16)] * 2 + [((BACK, cols, LANES), BF16)] * 2 + [((tiles, per, nch), BF16)],
        6,
        [
            VMEM((4, cells, LANES), BF16),
            VMEM((cells, hid), BF16),
            VMEM((cells, nch), BF16),
            VMEM((cells // 2, obs_n), BF16),
            VMEM((obs_n, 2 * nch), BF16),
            VMEM((4, cells, LANES), F32),
            VMEM((obs_n // LANES, META, LANES), F32),
            VMEM(got.shape, BF16),
            pltpu.SemaphoreType.DMA((1,)),
        ],
        (0,), 4 * cells * hid * (foot * LANES + nch), cells * hid * 4, far=(2,),
    )(
        jnp.array(arrangement_table(), jnp.int32), cols16, got, win, obs_out_weight,
        obs_precision[None, :],
    )
    back = lax.all_to_all(pred, ("lat", "lon"), split_axis=0, concat_axis=0, tiled=True)

    top, bottom, near, far = halo_rows(*rim)
    right, left = halo_columns(near, far)
    (derivative,) = call(
        functools.partial(adjoint_body, n_lat),
        [((v, rows, cols), F32)],
        15,
        [
            VMEM((rows + 2 * BACK, width // SUB + 2, SUB, ch), BF16),
            VMEM((rows + 2, width // SUB + 2, SUB, ch), BF16),
            VMEM((rows + 2 * BACK, width, ch), F32),
            VMEM((rows + 2, width, ch), F32),
            VMEM((rows + 2 * BACK, width, LANES), F32),
            VMEM((rows, width, LANES), F32),
            VMEM((LANES, ch), BF16),
            VMEM((LANES, ch), BF16),
            VMEM((8, LANES), F32),
            VMEM((rows, cols, LANES), F32),
            VMEM(slope0.shape, BF16),
            VMEM(slope1.shape, BF16),
            VMEM(w_fwd.shape, BF16),
            VMEM((v, rows, cols), F32),
            VMEM((v, rows, cols), F32),
            pltpu.SemaphoreType.DMA((7,)),
        ],
        (0,), 3 * conv_flops, cells * ch * 8, far=(6, 7, 8, 10, 12, 13),
    )(
        lat_id, adj16, top, bottom, right, left, adj, slope0, slope1, rot, w_fwd, encoder_weight,
        analysis_vector, prior_estimate, prior_precision[None, :],
    )
    (departures,) = call(
        unpack_body, [((obs_n, nch), F32)], 5, smem=(0, 1), moved=obs_n * nch * 10
    )(order, obs_count, back, obs_values, obs_precision[None, :])
    return departures, derivative


def solution(mesh):
    return jax.shard_map(
        on_device,
        mesh=mesh,
        in_specs=(
            P(None, "lat", "lon"),
            P(None, "lat", "lon"),
            P(),
            P(),
            P(),
            P(),
            P(),
            P(),
            P(("lat", "lon"), None),
            P(),
            P(("lat", "lon"), None),
            P(("lat", "lon")),
        ),
        out_specs=(P(("lat", "lon"), None), P(None, "lat", "lon")),
        check_vma=False,
    )
```

```python
import functools
import itertools

import jax
import jax.numpy as jnp
from jax import lax
from jax.experimental import pallas as pl
from jax.experimental.pallas import tpu as pltpu
from jax.sharding import PartitionSpec as P


F32 = jnp.float32
BF16 = jnp.bfloat16
LANES = 128
EDGE = 8
HALO = 4
BACK = 2
META = 8
CHUNK = 32
VMEM = pltpu.VMEM
SMEM = pltpu.SMEM


def call(body, outs, n_in, scratch=(), smem=(), flops=0, moved=0, limit=53, far=(), far_out=()):
    def spec(i, far=far, smem=smem):
        space = SMEM if i in smem else pltpu.HBM if i in far else VMEM
        return pl.BlockSpec(memory_space=space)

    specs = [spec(i) for i in range(n_in)]
    return pl.pallas_call(
        body,
        out_shape=tuple(jax.ShapeDtypeStruct(s, d) for s, d in outs),
        in_specs=specs,
        out_specs=tuple(spec(i, far_out, ()) for i in range(len(outs))),
        scratch_shapes=list(scratch),
        cost_estimate=pl.CostEstimate(flops=flops, bytes_accessed=moved, transcendentals=0),
        compiler_params=pltpu.CompilerParams(vmem_limit_bytes=limit * 2**20),
    )


def sigma(v):
    return 0.5 * jnp.tanh(0.5 * v) + 0.5


def dot(a, b):
    return jnp.dot(a, b, preferred_element_type=F32)


def dot_t(a, b):
    return lax.dot_general(a, b, (((1,), (1,)), ((), ())), preferred_element_type=F32)


def fetch(src, dst, sem):
    copy = pltpu.make_async_copy(src, dst, sem)
    copy.start()
    return copy


def padded(ref, src_ref):
    ref[...] = jnp.zeros_like(ref)
    ref[0 : src_ref.shape[0], :] = src_ref[...]


def edges(half, r, rows, width, first_ref, last_ref, head_ref, tail_ref):
    first_ref[r] = half[:EDGE]
    last_ref[r] = half[half.shape[0] - EDGE :]
    if r < width:
        head_ref[r] = half
    if r >= rows - width:
        tail_ref[r - rows + width] = half


def state_body(a_ref, at_ref, first_ref, last_ref, head_ref, tail_ref):
    v, rows, cols = a_ref.shape
    pad = jnp.zeros((LANES - v, cols), F32)
    for r in range(rows):
        x = jnp.concatenate([a_ref[:, r, :], pad], axis=0).T
        at_ref[r] = x
        edges(x.astype(BF16), r, rows, HALO, first_ref, last_ref, head_ref, tail_ref)


def sides_body(top_ref, bottom_ref, first_ref, last_ref, near_ref, far_ref):
    width, cols, _ = top_ref.shape
    rows = first_ref.shape[0]
    near_ref[0:width] = top_ref[:, :EDGE]
    near_ref[width : width + rows] = first_ref[...]
    near_ref[width + rows :] = bottom_ref[:, :EDGE]
    far_ref[0:width] = top_ref[:, cols - EDGE :]
    far_ref[width : width + rows] = last_ref[...]
    far_ref[width + rows :] = bottom_ref[:, cols - EDGE :]


def pack_body(order_ref, obs_ref, meta_ref, out_ref):
    tiles = out_ref.shape[0]
    per = out_ref.shape[1] - META

    def one(p, c):
        h = order_ref[p]
        out_ref[h, 0:per, :] = obs_ref[pl.ds(p, per, stride=tiles), :].astype(BF16)
        return c

    lax.fori_loop(0, tiles, one, 0, unroll=8)
    for h in range(tiles):
        out_ref[h, per : per + META, :] = meta_ref[h]


def unpack_body(order_ref, count_ref, got_ref, obs_ref, prec_ref, out_ref):
    tiles, per, _ = got_ref.shape
    prec = prec_ref[...]
    slot = (lax.broadcasted_iota(jnp.int32, (per, LANES), 0) + pl.program_id(0) * per) * tiles
    for p in range(tiles):
        at = pl.ds(p, per, stride=tiles)
        dep = (got_ref[order_ref[p]].astype(F32) - obs_ref[at, :]) * prec
        out_ref[at, :] = jnp.where(slot + p < count_ref[0], dep, 0.0)


def unpack(order, count, got, obs, prec):
    tiles, per, nch = got.shape
    chunk = min(per, CHUNK)
    rows = pl.BlockSpec((chunk * tiles, nch), lambda k: (k, 0))
    small = pl.BlockSpec(memory_space=SMEM)
    return pl.pallas_call(
        unpack_body,
        grid=(per // chunk,),
        out_shape=jax.ShapeDtypeStruct(obs.shape, F32),
        in_specs=[
            small,
            small,
            pl.BlockSpec((tiles, chunk, nch), lambda k: (0, k, 0)),
            rows,
            pl.BlockSpec((1, nch), lambda k: (0, 0)),
        ],
        out_specs=rows,
        compiler_params=pltpu.CompilerParams(vmem_limit_bytes=53 * 2**20),
        name="unpack",
    )(order, count, got, obs, prec)


def shift_pairs(size, wrap):
    up = [(i, (i + 1) % size) for i in range(size if wrap else size - 1)]
    return up, [(j, i) for i, j in up]


def halo_rows(first, last, head, tail):
    up, down = shift_pairs(lax.axis_size("lat"), False)
    top = lax.ppermute(tail, "lat", up)
    bottom = lax.ppermute(head, "lat", down)
    shape = (first.shape[0] + 2 * head.shape[0],) + first.shape[1:]
    near, far = call(sides_body, [(shape, BF16)] * 2, 4)(
        top, bottom, first, last
    )
    return top, bottom, near, far


def halo_columns(near, far):
    up, down = shift_pairs(lax.axis_size("lon"), True)
    left = lax.ppermute(far, "lon", up)
    right = lax.ppermute(near, "lon", down)
    return right, left


def bands(mid_ref, top_ref, bottom_ref, width):
    rows = mid_ref.shape[0]
    return (
        [(top_ref, r) for r in range(width)]
        + [(mid_ref, r) for r in range(rows)]
        + [(bottom_ref, r) for r in range(width)]
    )


def fold_row(nat_ref, e, q_n):
    slabs = [nat_ref[e, pl.ds(q, SUB, stride=q_n), :] for q in range(q_n)]
    return jnp.concatenate(slabs, axis=0)


def unfold_row(nat_ref, e, value, q_n):
    for q in range(q_n):
        nat_ref[e, pl.ds(q, SUB, stride=q_n), :] = value[q * SUB : (q + 1) * SUB]


def put_row(ref, e, value):
    n, ch = value.shape
    q_n = n // SUB
    ref[e, 1 : q_n + 1] = value.astype(BF16).reshape(q_n, SUB, ch)
    ref[e, 0] = pltpu.roll(value[n - SUB :], 1, 0).astype(BF16)
    ref[e, q_n + 1] = pltpu.roll(value[:SUB], SUB - 1, 0).astype(BF16)


def center(ref, e):
    q_n, ch = ref.shape[1] - 2, ref.shape[3]
    return ref[e, 1 : q_n + 1].reshape(q_n * SUB, ch)


def conv_rows(ref, e, count, weight):
    q_n, ch = ref.shape[1] - 2, ref.shape[3]
    parts = [
        ref[e + i : e + i + count, j : j + q_n].reshape(count * q_n * SUB, ch)
        for i in range(3)
        for j in range(3)
    ]
    return dot(jnp.concatenate(parts, axis=1), weight)


def conv_back(ref, e, count, weight_ref):
    q_n, ch = ref.shape[1] - 2, ref.shape[3]
    parts = [
        ref[e + i : e + i + count, j : j + q_n].reshape(count * q_n * SUB, ch)
        for i in range(3)
        for j in range(3)
    ]
    taps = [weight_ref[(8 - t) * ch : (9 - t) * ch, :] for t in range(9)]
    return dot_t(jnp.concatenate(parts, axis=1), jnp.concatenate(taps, axis=1))


def inside(lat_ref, a, rows, n_lat):
    g = lat_ref[0] * rows + a
    return jnp.logical_and(g >= 0, g < n_lat * rows)


STEP = 2
SUB = 16


def forward_body(
    n_lat, lat_ref, top_ref, bottom_ref, right_ref, left_ref, at_ref, enc_in, w_ref, ro_in,
    cols_ref, slope0_out, slope1_out,
    a0, a1, nat, back, enc_ref, ro_ref, w_v, at_v, slope0_ref, slope1_ref, sem,
):
    at_in = fetch(at_ref, at_v, sem.at[2])
    w0 = fetch(w_ref.at[0], w_v.at[0], sem.at[0])
    w1 = fetch(w_ref.at[1], w_v.at[1], sem.at[1])
    padded(enc_ref, enc_in)
    padded(ro_ref, ro_in)
    rows, cols, _ = at_v.shape
    at_in.wait()
    q_n = a0.shape[1] - 2
    n = q_n * SUB
    for e, (src, r) in enumerate(bands(at_v, top_ref, bottom_ref, HALO)):
        nat[e, 0:cols, :] = src[r].astype(F32)
        nat[e, cols : cols + EDGE, :] = right_ref[e].astype(F32)
        nat[e, cols + EDGE :, :] = left_ref[e].astype(F32)
        x = fold_row(nat, e, q_n).astype(BF16)
        put_row(a0, e, dot(x, enc_ref[...]))

    def first(e):
        pre = conv_rows(a0, e, STEP, w_v[0])
        s = sigma(pre)
        act = pre * s
        slope = (s + act * (1.0 - s)).astype(BF16)
        for q in range(STEP):
            at = slice(q * n, (q + 1) * n)
            slope0_ref[e + q] = slope[at]
            h = center(a0, e + q + 1).astype(F32) + act[at]
            a = e + q - HALO + 1
            if a < 0 or a >= rows:
                h = jnp.where(inside(lat_ref, a, rows, n_lat), h, 0.0)
            put_row(a1, e + q, h)

    def second(e):
        pre = conv_rows(a1, e, STEP, w_v[1])
        s = sigma(pre)
        act = pre * s
        slope = (s + act * (1.0 - s)).astype(BF16)
        for q in range(STEP):
            at = slice(q * n, (q + 1) * n)
            slope1_ref[e + q] = slope[at]
            a = e + q - HALO + 2
            if 0 <= a < rows:
                h = center(a1, e + q + 1).astype(F32) + act[at]
                unfold_row(back, a, dot_t(h.astype(BF16), ro_ref[...]), q_n)
                cols_ref[a] = (at_v[a] + back[a, 0:cols, :]).astype(BF16)

    w0.wait()
    for e in range(0, rows + 2 * HALO - 2, STEP):
        first(e)
    out0 = fetch(slope0_ref, slope0_out, sem.at[3])
    w1.wait()
    half = (rows + 2 * HALO - 4) // 2
    for e in range(0, half, STEP):
        second(e)
    out1 = fetch(slope1_ref.at[0:half], slope1_out.at[0:half], sem.at[4])
    for e in range(half, 2 * half, STEP):
        second(e)
    out2 = fetch(slope1_ref.at[half:], slope1_out.at[half:], sem.at[5])
    out0.wait()
    out1.wait()
    out2.wait()


def adjoint_body(
    n_lat, lat_ref, top_ref, bottom_ref, right_ref, left_ref, adj_in, slope0_in, slope1_in,
    rot_in, w_in, enc_in, state_in, prior_in, prec_in,
    out_ref, b1, b0, adj2, adj1, nat, back, rot_ref, enc_ref, prec_pad,
    adj_ref, slope0_ref, slope1_ref, w_ref, state_ref, prior_ref, sem,
):
    adj_got = fetch(adj_in, adj_ref, sem.at[4])
    slope1_got = fetch(slope1_in, slope1_ref, sem.at[0])
    w1 = fetch(w_in.at[1], w_ref.at[1], sem.at[1])
    slope0_got = fetch(slope0_in, slope0_ref, sem.at[2])
    w0 = fetch(w_in.at[0], w_ref.at[0], sem.at[3])
    late = [
        fetch(state_in, state_ref, sem.at[5]),
        fetch(prior_in, prior_ref, sem.at[6]),
    ]
    padded(rot_ref, rot_in)
    padded(enc_ref, enc_in)
    prec_pad[...] = jnp.zeros_like(prec_pad)
    prec_pad[0:1, 0 : prec_in.shape[1]] = prec_in[...]
    rows, cols, _ = adj_ref.shape
    q_n = b1.shape[1] - 2
    n = q_n * SUB
    v = out_ref.shape[0]
    prec = jnp.broadcast_to(prec_pad[0:1, :], (LANES, LANES)).T[0:v, :]
    adj_got.wait()
    slope1_got.wait()
    for e, (src, r) in enumerate(bands(adj_ref, top_ref, bottom_ref, BACK)):
        nat[e, 0:cols, :] = src[r].astype(F32)
        nat[e, cols : cols + EDGE, :] = right_ref[e].astype(F32)
        nat[e, cols + EDGE :, :] = left_ref[e].astype(F32)
        g = dot(fold_row(nat, e, q_n).astype(BF16), rot_ref[...])
        adj2[e] = g
        put_row(b1, e, g * slope1_ref[e].astype(F32))

    slope0_got.wait()
    w1.wait()
    for e in range(0, rows + 2, STEP):
        g = conv_back(b1, e, STEP, w_ref.at[1])
        for q in range(STEP):
            total = adj2[e + q + 1] + g[q * n : (q + 1) * n]
            adj1[e + q] = total
            h = total * slope0_ref[e + q + 2].astype(F32)
            a = e + q - 1
            if a < 0 or a >= rows:
                h = jnp.where(inside(lat_ref, a, rows, n_lat), h, 0.0)
            put_row(b0, e + q, h)

    w0.wait()
    for copy in late:
        copy.wait()
    for a in range(0, rows, STEP):
        g = conv_back(b0, a, STEP, w_ref.at[0])
        for q in range(STEP):
            total = adj1[a + q + 1] + g[q * n : (q + 1) * n]
            unfold_row(back, a + q, dot_t(total.astype(BF16), enc_ref[...]), q_n)
            grow = back[a + q, 0:cols, :] + adj_ref[a + q]
            diff = state_ref[:, a + q, :] - prior_ref[:, a + q, :]
            out_ref[:, a + q, :] = prec * diff + grow.T[0:v, :]


BLOCK = 1024


def observe_body(
    table_ref, cols_ref, got_in, win_ref, wout_ref, prec_ref,
    adj_ref, first_ref, last_ref, head_ref, tail_ref, pred_ref,
    xs, slope, grid, hot, weights, fa, meta, got_ref, sem,
):
    got = fetch(got_in, got_ref, sem.at[0])
    rows, cols, _ = cols_ref.shape
    cells = rows * cols
    half = cells // 2
    tiles, per, nch = pred_ref.shape
    obs_n = tiles * per
    group = LANES // per
    prec2 = prec_ref[...] * prec_ref[...]
    c0 = cols_ref[...].reshape(cells, LANES)
    c1 = pltpu.roll(c0.astype(F32), cells - 1, 0).astype(BF16)
    xs[0] = c0
    xs[1] = c1
    xs[2] = jnp.concatenate([c0[cols:], c0[:cols]], axis=0)
    xs[3] = jnp.concatenate([c1[cols:], c1[:cols]], axis=0)
    rest = jnp.zeros((1, LANES), F32)
    got.wait()
    for m in range(obs_n // LANES):
        total = got_ref[m * group, per : per + META, :].astype(F32)
        for g in range(1, group):
            total += got_ref[m * group + g, per : per + META, :].astype(F32)
        meta[m] = total
        rest += jnp.where(total[2:3] == table_ref[0, 4].astype(F32), 0.0, 1.0)
    trips = jnp.where(jnp.sum(rest) > 0.0, table_ref.shape[0], 1)
    fa[...] = jnp.zeros_like(fa)

    def arrangement(cls, carry):
        place = [table_ref[cls, f] for f in range(4)]
        code = table_ref[cls, 4].astype(F32)

        def forward(k, c):
            at = pl.ds(k * BLOCK, BLOCK)
            x = jnp.concatenate([xs[place[f], at, :] for f in range(4)], axis=1)
            inner = dot(x, win_ref[...])
            s = sigma(inner)
            act = inner * s
            slope[at, :] = (s + act * (1.0 - s)).astype(BF16)
            grid[at, :] = dot(act.astype(BF16), wout_ref[...]).astype(BF16)
            return c

        lax.fori_loop(0, cells // BLOCK, forward, 0)
        both = jnp.concatenate([grid[0:half, :], grid[half:, :]], axis=1)
        lane = lax.broadcasted_iota(jnp.int32, (LANES, LANES), 1).astype(F32)
        sub = lax.broadcasted_iota(jnp.int32, (LANES, LANES), 0).astype(F32)
        top = float(rows // 2)
        one16, zero16 = jnp.ones((LANES, LANES), BF16), jnp.zeros((LANES, LANES), BF16)

        def gather(m, c):
            mine = meta[m, 2:3, :] == code
            row = jnp.broadcast_to(jnp.where(mine, meta[m, 0:1, :], float(rows)), (LANES, LANES))
            col = jnp.broadcast_to(meta[m, 1:2, :], (LANES, LANES))
            row_t, col_t = row.T, col.T
            local = jnp.where(row_t < top, row_t, row_t - top)
            value = jnp.where(col_t == lane, local, -1.0).astype(BF16)
            sel = jnp.concatenate(
                [jnp.where(value == jnp.asarray(t, BF16), one16, zero16) for t in range(rows // 2)],
                axis=1,
            )
            out = dot(sel, both)
            upper = row_t >= top
            pred = jnp.where(upper, out[:, nch:], out[:, :nch])
            pred = jnp.where(row_t < float(rows), pred, 0.0)
            obs = got_ref[pl.ds(m * group, group), 0:per, :].astype(F32).reshape(LANES, nch)
            w = (pred - obs) * prec2
            at = pl.ds(m * LANES, LANES)
            weights[at, 0:nch] = jnp.where(upper, 0.0, w).astype(BF16)
            weights[at, nch:] = jnp.where(upper, w, 0.0).astype(BF16)
            pred = pred.reshape(group, per, nch)
            where = pl.ds(m * group, group)

            before = jnp.where(cls > 0, pred_ref[where].astype(F32), 0.0)
            pred_ref[where] = (before + pred).astype(BF16)
            local = jnp.where(row < top, row, row - top)
            value = jnp.where(col == sub, local, -1.0).astype(BF16)
            for t in range(rows // 2):
                hot[t * LANES : (t + 1) * LANES, pl.ds(pl.multiple_of(m * LANES, LANES), LANES)] = (
                    jnp.where(value == jnp.asarray(t, BF16), one16, zero16)
                )
            return c

        lax.fori_loop(0, obs_n // LANES, gather, 0, unroll=4)

        def scatter(k, c):
            at = pl.ds(k * BLOCK, BLOCK)
            total = dot(hot[at, :], weights[...])
            grid[at, :] = total[:, :nch].astype(BF16)
            grid[pl.ds(half + k * BLOCK, BLOCK), :] = total[:, nch:].astype(BF16)
            return c

        lax.fori_loop(0, half // BLOCK, scatter, 0)

        def backward(k, c):
            at = pl.ds(k * BLOCK, BLOCK)
            act = dot_t(grid[at, :], wout_ref[...])
            inner = (act * slope[at, :].astype(F32)).astype(BF16)
            x = dot_t(inner, win_ref[...])
            for f in range(4):
                fa[place[f], at, :] += x[:, f * LANES : (f + 1) * LANES]
            return c

        lax.fori_loop(0, cells // BLOCK, backward, 0)
        return carry

    lax.fori_loop(0, trips, arrangement, 0)
    high = fa[3]
    one = fa[1] + jnp.concatenate([high[cells - cols :], high[: cells - cols]], axis=0)
    low = fa[2]
    total = fa[0] + jnp.concatenate([low[cells - cols :], low[: cells - cols]], axis=0)
    total += pltpu.roll(one, 1, 0)
    total = total.reshape(rows, cols, LANES)
    adj_ref[...] = total
    total = total.astype(BF16)
    for r in range(rows):
        edges(total[r], r, rows, BACK, first_ref, last_ref, head_ref, tail_ref)


def arrangement_table():
    orders = list(itertools.permutations(range(4)))
    first = (0, 2, 1, 3)
    orders.remove(first)
    return [
        list(o) + [sum(q * 4**f for f, q in enumerate(o))] for o in [first] + orders
    ]


def on_device(
    analysis_vector,
    prior_estimate,
    prior_precision,
    encoder_weight,
    conv_weights,
    readout_matrix,
    obs_in_weight,
    obs_out_weight,
    obs_values,
    obs_precision,
    foot_cells,
    obs_count,
):
    v, rows, cols = analysis_vector.shape
    n_lat, n_lon = lax.axis_size("lat"), lax.axis_size("lon")
    tiles = n_lat * n_lon
    obs_n, foot = foot_cells.shape
    per = obs_n // tiles
    ch = encoder_weight.shape[1]
    hid, nch = obs_out_weight.shape
    width = cols + 2 * EDGE
    cells = rows * cols
    lat, lon = lax.axis_index("lat"), lax.axis_index("lon")
    lat_id = lat.reshape(1)

    strip = (rows, EDGE, LANES)
    at, *rim = call(
        state_body,
        [((rows, cols, LANES), F32)]
        + [(strip, BF16)] * 2 + [((HALO, cols, LANES), BF16)] * 2,
        1, moved=cells * v * 8,
    )(analysis_vector)
    foot_cells, obs_sent, *rim = lax.optimization_barrier((foot_cells, obs_values, *rim))
    top, bottom, near, far = halo_rows(*rim)

    lon_total = cols * n_lon
    lat_g, lon_g = foot_cells // lon_total, foot_cells % lon_total
    order = lat_g[:tiles, 0] // rows * n_lon + lon_g[:tiles, 0] // cols
    base_lat, base_lon = jnp.min(lat_g, axis=1), jnp.min(lon_g, axis=1)
    place = (lat_g - base_lat[:, None]) * 2 + (lon_g - base_lon[:, None])
    code = jnp.sum(place * (4 ** jnp.arange(foot)), axis=1)
    valid = jnp.arange(obs_n) < obs_count[0]
    local = jnp.where(valid, base_lat % rows, rows)
    fields = jnp.stack([local, base_lon % cols, code]).astype(BF16).reshape(3, per, tiles)
    pick = (order[None, :] == jnp.arange(tiles)[:, None]).astype(BF16)
    meta = jnp.einsum("fkp,hp->hfk", fields, pick, preferred_element_type=F32).astype(BF16)
    group = LANES // per
    mine = jnp.arange(group) == (lat * n_lon + lon) % group
    meta = jnp.where(mine[:, None], meta[:, :, None, :], jnp.zeros((), BF16)).reshape(tiles, 3, LANES)
    meta = jnp.pad(meta, ((0, 0), (0, META - 3), (0, 0)))
    (send,) = call(
        pack_body, [((tiles, per + META, nch), BF16)], 3, smem=(0,), moved=obs_n * nch * 6
    )(order, obs_sent, meta)
    send, near, far = lax.optimization_barrier((send, near, far))
    right, left = halo_columns(near, far)
    got = lax.all_to_all(send, ("lat", "lon"), split_axis=0, concat_axis=0, tiled=True)

    rot = readout_matrix.T
    win = jnp.pad(obs_in_weight, ((0, 0), (0, LANES - v), (0, 0))).reshape(foot * LANES, hid)
    w_fwd = conv_weights.reshape(conv_weights.shape[0], 9 * ch, ch)

    conv_flops = 2 * cells * 9 * ch * ch
    cols16, slope0, slope1 = call(
        functools.partial(forward_body, n_lat),
        [
            ((rows, cols, LANES), BF16),
            ((rows + 2 * HALO - 2, width, ch), BF16),
            ((rows + 2 * HALO - 4, width, ch), BF16),
        ],
        9,
        [
            VMEM((rows + 2 * HALO, width // SUB + 2, SUB, ch), BF16),
            VMEM((rows + 2 * HALO - 2, width // SUB + 2, SUB, ch), BF16),
            VMEM((rows + 2 * HALO, width, LANES), F32),
            VMEM((rows, width, LANES), F32),
            VMEM((LANES, ch), BF16),
            VMEM((LANES, ch), BF16),
            VMEM(w_fwd.shape, BF16),
            VMEM((rows, cols, LANES), F32),
            VMEM((rows + 2 * HALO - 2, width, ch), BF16),
            VMEM((rows + 2 * HALO - 4, width, ch), BF16),
            pltpu.SemaphoreType.DMA((6,)),
        ],
        (0,), 3 * conv_flops, cells * ch * 8, far=(5, 7), far_out=(1, 2),
    )(lat_id, top, bottom, right, left, at, encoder_weight, w_fwd, rot)

    adj, *rim, pred = call(
        observe_body,
        [((rows, cols, LANES), F32)]
        + [(strip, BF16)] * 2 + [((BACK, cols, LANES), BF16)] * 2 + [((tiles, per, nch), BF16)],
        6,
        [
            VMEM((4, cells, LANES), BF16),
            VMEM((cells, hid), BF16),
            VMEM((cells, nch), BF16),
            VMEM((cells // 2, obs_n), BF16),
            VMEM((obs_n, 2 * nch), BF16),
            VMEM((4, cells, LANES), F32),
            VMEM((obs_n // LANES, META, LANES), F32),
            VMEM(got.shape, BF16),
            pltpu.SemaphoreType.DMA((1,)),
        ],
        (0,), 4 * cells * hid * (foot * LANES + nch), cells * hid * 4, limit=50, far=(2,),
    )(
        jnp.array(arrangement_table(), jnp.int32), cols16, got, win, obs_out_weight,
        obs_precision[None, :],
    )
    back = lax.all_to_all(pred, ("lat", "lon"), split_axis=0, concat_axis=0, tiled=True)

    top, bottom, near, far = halo_rows(*rim)
    right, left = halo_columns(near, far)
    (derivative,) = call(
        functools.partial(adjoint_body, n_lat),
        [((v, rows, cols), F32)],
        14,
        [
            VMEM((rows + 2 * BACK, width // SUB + 2, SUB, ch), BF16),
            VMEM((rows + 2, width // SUB + 2, SUB, ch), BF16),
            VMEM((rows + 2 * BACK, width, ch), F32),
            VMEM((rows + 2, width, ch), F32),
            VMEM((rows + 2 * BACK, width, LANES), F32),
            VMEM((rows, width, LANES), F32),
            VMEM((LANES, ch), BF16),
            VMEM((LANES, ch), BF16),
            VMEM((8, LANES), F32),
            VMEM((rows, cols, LANES), F32),
            VMEM(slope0.shape, BF16),
            VMEM(slope1.shape, BF16),
            VMEM(w_fwd.shape, BF16),
            VMEM((v, rows, cols), F32),
            VMEM((v, rows, cols), F32),
            pltpu.SemaphoreType.DMA((7,)),
        ],
        (0,), 3 * conv_flops, cells * ch * 8, far=(5, 6, 7, 9, 11, 12),
    )(
        lat_id, top, bottom, right, left, adj, slope0, slope1, rot, w_fwd, encoder_weight,
        analysis_vector, prior_estimate, prior_precision[None, :],
    )
    departures = unpack(order, obs_count, back, obs_values, obs_precision[None, :])
    return departures, derivative


def solution(mesh):
    return jax.shard_map(
        on_device,
        mesh=mesh,
        in_specs=(
            P(None, "lat", "lon"),
            P(None, "lat", "lon"),
            P(),
            P(),
            P(),
            P(),
            P(),
            P(),
            P(("lat", "lon"), None),
            P(),
            P(("lat", "lon"), None),
            P(("lat", "lon")),
        ),
        out_specs=(P(("lat", "lon"), None), P(None, "lat", "lon")),
        check_vma=False,
    )
```

```python
import functools
import itertools

import jax
import jax.numpy as jnp
from jax import lax
from jax.experimental import pallas as pl
from jax.experimental.pallas import tpu as pltpu
from jax.sharding import PartitionSpec as P


F32 = jnp.float32
BF16 = jnp.bfloat16
LANES = 128
EDGE = 8
HALO = 4
BACK = 2
META = 8
CHUNK = 32
VMEM = pltpu.VMEM
SMEM = pltpu.SMEM


def call(body, outs, n_in, scratch=(), smem=(), flops=0, moved=0, limit=53, far=(), far_out=()):
    def spec(i, far=far, smem=smem):
        space = SMEM if i in smem else pltpu.HBM if i in far else VMEM
        return pl.BlockSpec(memory_space=space)

    specs = [spec(i) for i in range(n_in)]
    return pl.pallas_call(
        body,
        out_shape=tuple(jax.ShapeDtypeStruct(s, d) for s, d in outs),
        in_specs=specs,
        out_specs=tuple(spec(i, far_out, ()) for i in range(len(outs))),
        scratch_shapes=list(scratch),
        cost_estimate=pl.CostEstimate(flops=flops, bytes_accessed=moved, transcendentals=0),
        compiler_params=pltpu.CompilerParams(vmem_limit_bytes=limit * 2**20),
    )


def sigma(v):
    return 0.5 * jnp.tanh(0.5 * v) + 0.5


def dot(a, b):
    return jnp.dot(a, b, preferred_element_type=F32)


def dot_t(a, b):
    return lax.dot_general(a, b, (((1,), (1,)), ((), ())), preferred_element_type=F32)


def fetch(src, dst, sem):
    copy = pltpu.make_async_copy(src, dst, sem)
    copy.start()
    return copy


def padded(ref, src_ref):
    ref[...] = jnp.zeros_like(ref)
    ref[0 : src_ref.shape[0], :] = src_ref[...]


def edges(half, r, rows, width, first_ref, last_ref, head_ref, tail_ref):
    first_ref[r] = half[:EDGE]
    last_ref[r] = half[half.shape[0] - EDGE :]
    if r < width:
        head_ref[r] = half
    if r >= rows - width:
        tail_ref[r - rows + width] = half


def state_body(a_ref, at_ref, first_ref, last_ref, head_ref, tail_ref):
    v, rows, cols = a_ref.shape
    pad = jnp.zeros((LANES - v, cols), F32)
    for r in range(rows):
        x = jnp.concatenate([a_ref[:, r, :], pad], axis=0).T
        at_ref[r] = x
        edges(x.astype(BF16), r, rows, HALO, first_ref, last_ref, head_ref, tail_ref)


def sides_body(top_ref, bottom_ref, first_ref, last_ref, near_ref, far_ref):
    width, cols, _ = top_ref.shape
    rows = first_ref.shape[0]
    near_ref[0:width] = top_ref[:, :EDGE]
    near_ref[width : width + rows] = first_ref[...]
    near_ref[width + rows :] = bottom_ref[:, :EDGE]
    far_ref[0:width] = top_ref[:, cols - EDGE :]
    far_ref[width : width + rows] = last_ref[...]
    far_ref[width + rows :] = bottom_ref[:, cols - EDGE :]


def pack_body(order_ref, obs_ref, meta_ref, out_ref, kept_ref):
    tiles = out_ref.shape[0]
    per = out_ref.shape[1] - META

    def one(p, c):
        h = order_ref[p]
        obs = obs_ref[pl.ds(p, per, stride=tiles), :]
        kept_ref[h] = obs
        out_ref[h, 0:per, :] = obs.astype(BF16)
        return c

    lax.fori_loop(0, tiles, one, 0, unroll=8)
    for h in range(tiles):
        out_ref[h, per : per + META, :] = meta_ref[h]


def unpack_body(order_ref, count_ref, got_ref, obs_ref, prec_ref, out_ref):
    tiles, per, _ = got_ref.shape
    prec = prec_ref[...]
    slot = (lax.broadcasted_iota(jnp.int32, (per, LANES), 0) + pl.program_id(0) * per) * tiles
    for p in range(tiles):
        at = pl.ds(p, per, stride=tiles)
        h = order_ref[p]
        dep = (got_ref[h].astype(F32) - obs_ref[h]) * prec
        out_ref[at, :] = jnp.where(slot + p < count_ref[0], dep, 0.0)


def unpack(order, count, got, obs, prec):
    tiles, per, nch = got.shape
    chunk = min(per, CHUNK)
    rows = pl.BlockSpec((tiles, chunk, nch), lambda k: (0, k, 0))
    small = pl.BlockSpec(memory_space=SMEM)
    return pl.pallas_call(
        unpack_body,
        grid=(per // chunk,),
        out_shape=jax.ShapeDtypeStruct((tiles * per, nch), F32),
        in_specs=[
            small,
            small,
            rows,
            rows,
            pl.BlockSpec((1, nch), lambda k: (0, 0)),
        ],
        out_specs=pl.BlockSpec((chunk * tiles, nch), lambda k: (k, 0)),
        compiler_params=pltpu.CompilerParams(vmem_limit_bytes=53 * 2**20),
        name="unpack",
    )(order, count, got, obs, prec)


def shift_pairs(size, wrap):
    up = [(i, (i + 1) % size) for i in range(size if wrap else size - 1)]
    return up, [(j, i) for i, j in up]


def halo_rows(first, last, head, tail):
    up, down = shift_pairs(lax.axis_size("lat"), False)
    top = lax.ppermute(tail, "lat", up)
    bottom = lax.ppermute(head, "lat", down)
    shape = (first.shape[0] + 2 * head.shape[0],) + first.shape[1:]
    near, far = call(sides_body, [(shape, BF16)] * 2, 4)(
        top, bottom, first, last
    )
    return top, bottom, near, far


def halo_columns(near, far):
    up, down = shift_pairs(lax.axis_size("lon"), True)
    left = lax.ppermute(far, "lon", up)
    right = lax.ppermute(near, "lon", down)
    return right, left


def bands(mid_ref, top_ref, bottom_ref, width):
    rows = mid_ref.shape[0]
    return (
        [(top_ref, r) for r in range(width)]
        + [(mid_ref, r) for r in range(rows)]
        + [(bottom_ref, r) for r in range(width)]
    )


def fold_row(nat_ref, e, q_n):
    slabs = [nat_ref[e, pl.ds(q, SUB, stride=q_n), :] for q in range(q_n)]
    return jnp.concatenate(slabs, axis=0)


def unfold_row(nat_ref, e, value, q_n):
    for q in range(q_n):
        nat_ref[e, pl.ds(q, SUB, stride=q_n), :] = value[q * SUB : (q + 1) * SUB]


def put_row(ref, e, value):
    n, ch = value.shape
    q_n = n // SUB
    ref[e, 1 : q_n + 1] = value.astype(BF16).reshape(q_n, SUB, ch)
    ref[e, 0] = pltpu.roll(value[n - SUB :], 1, 0).astype(BF16)
    ref[e, q_n + 1] = pltpu.roll(value[:SUB], SUB - 1, 0).astype(BF16)


def center(ref, e):
    q_n, ch = ref.shape[1] - 2, ref.shape[3]
    return ref[e, 1 : q_n + 1].reshape(q_n * SUB, ch)


def conv_rows(ref, e, count, weight):
    q_n, ch = ref.shape[1] - 2, ref.shape[3]
    parts = [
        ref[e + i : e + i + count, j : j + q_n].reshape(count * q_n * SUB, ch)
        for i in range(3)
        for j in range(3)
    ]
    return dot(jnp.concatenate(parts, axis=1), weight)


def conv_back(ref, e, count, weight_ref):
    q_n, ch = ref.shape[1] - 2, ref.shape[3]
    parts = [
        ref[e + i : e + i + count, j : j + q_n].reshape(count * q_n * SUB, ch)
        for i in range(3)
        for j in range(3)
    ]
    taps = [weight_ref[(8 - t) * ch : (9 - t) * ch, :] for t in range(9)]
    return dot_t(jnp.concatenate(parts, axis=1), jnp.concatenate(taps, axis=1))


def inside(lat_ref, a, rows, n_lat):
    g = lat_ref[0] * rows + a
    return jnp.logical_and(g >= 0, g < n_lat * rows)


STEP = 2
SUB = 16


def forward_body(
    n_lat, lat_ref, top_ref, bottom_ref, right_ref, left_ref, at_ref, enc_in, w_ref, ro_in,
    cols_ref, slope0_out, slope1_out,
    a0, a1, nat, back, enc_ref, ro_ref, w_v, at_v, slope0_ref, slope1_ref, sem,
):
    at_in = fetch(at_ref, at_v, sem.at[2])
    w0 = fetch(w_ref.at[0], w_v.at[0], sem.at[0])
    w1 = fetch(w_ref.at[1], w_v.at[1], sem.at[1])
    padded(enc_ref, enc_in)
    padded(ro_ref, ro_in)
    rows, cols, _ = at_v.shape
    at_in.wait()
    q_n = a0.shape[1] - 2
    n = q_n * SUB
    for e, (src, r) in enumerate(bands(at_v, top_ref, bottom_ref, HALO)):
        nat[e, 0:cols, :] = src[r].astype(F32)
        nat[e, cols : cols + EDGE, :] = right_ref[e].astype(F32)
        nat[e, cols + EDGE :, :] = left_ref[e].astype(F32)
        x = fold_row(nat, e, q_n).astype(BF16)
        put_row(a0, e, dot(x, enc_ref[...]))

    def first(e):
        pre = conv_rows(a0, e, STEP, w_v[0])
        s = sigma(pre)
        act = pre * s
        slope = (s + act * (1.0 - s)).astype(BF16)
        for q in range(STEP):
            at = slice(q * n, (q + 1) * n)
            slope0_ref[e + q] = slope[at]
            h = center(a0, e + q + 1).astype(F32) + act[at]
            a = e + q - HALO + 1
            if a < 0 or a >= rows:
                h = jnp.where(inside(lat_ref, a, rows, n_lat), h, 0.0)
            put_row(a1, e + q, h)

    def second(e):
        pre = conv_rows(a1, e, STEP, w_v[1])
        s = sigma(pre)
        act = pre * s
        slope = (s + act * (1.0 - s)).astype(BF16)
        for q in range(STEP):
            at = slice(q * n, (q + 1) * n)
            slope1_ref[e + q] = slope[at]
            a = e + q - HALO + 2
            if 0 <= a < rows:
                h = center(a1, e + q + 1).astype(F32) + act[at]
                unfold_row(back, a, dot_t(h.astype(BF16), ro_ref[...]), q_n)
                cols_ref[a] = (at_v[a] + back[a, 0:cols, :]).astype(BF16)

    w0.wait()
    for e in range(0, rows + 2 * HALO - 2, STEP):
        first(e)
    out0 = fetch(slope0_ref, slope0_out, sem.at[3])
    w1.wait()
    half = (rows + 2 * HALO - 4) // 2
    for e in range(0, half, STEP):
        second(e)
    out1 = fetch(slope1_ref.at[0:half], slope1_out.at[0:half], sem.at[4])
    for e in range(half, 2 * half, STEP):
        second(e)
    out2 = fetch(slope1_ref.at[half:], slope1_out.at[half:], sem.at[5])
    out0.wait()
    out1.wait()
    out2.wait()


def adjoint_body(
    n_lat, lat_ref, top_ref, bottom_ref, right_ref, left_ref, adj_in, slope0_in, slope1_in,
    rot_in, w_in, enc_in, state_in, prior_in, prec_in,
    out_ref, b1, b0, adj2, adj1, nat, back, rot_ref, enc_ref, prec_pad,
    adj_ref, slope0_ref, slope1_ref, w_ref, state_ref, prior_ref, sem,
):
    adj_got = fetch(adj_in, adj_ref, sem.at[4])
    slope1_got = fetch(slope1_in, slope1_ref, sem.at[0])
    w1 = fetch(w_in.at[1], w_ref.at[1], sem.at[1])
    slope0_got = fetch(slope0_in, slope0_ref, sem.at[2])
    w0 = fetch(w_in.at[0], w_ref.at[0], sem.at[3])
    late = [
        fetch(state_in, state_ref, sem.at[5]),
        fetch(prior_in, prior_ref, sem.at[6]),
    ]
    padded(rot_ref, rot_in)
    padded(enc_ref, enc_in)
    prec_pad[...] = jnp.zeros_like(prec_pad)
    prec_pad[0:1, 0 : prec_in.shape[1]] = prec_in[...]
    rows, cols, _ = adj_ref.shape
    q_n = b1.shape[1] - 2
    n = q_n * SUB
    v = out_ref.shape[0]
    prec = jnp.broadcast_to(prec_pad[0:1, :], (LANES, LANES)).T[0:v, :]
    adj_got.wait()
    slope1_got.wait()
    for e, (src, r) in enumerate(bands(adj_ref, top_ref, bottom_ref, BACK)):
        nat[e, 0:cols, :] = src[r].astype(F32)
        nat[e, cols : cols + EDGE, :] = right_ref[e].astype(F32)
        nat[e, cols + EDGE :, :] = left_ref[e].astype(F32)
        g = dot(fold_row(nat, e, q_n).astype(BF16), rot_ref[...])
        adj2[e] = g
        put_row(b1, e, g * slope1_ref[e].astype(F32))

    slope0_got.wait()
    w1.wait()
    for e in range(0, rows + 2, STEP):
        g = conv_back(b1, e, STEP, w_ref.at[1])
        for q in range(STEP):
            total = adj2[e + q + 1] + g[q * n : (q + 1) * n]
            adj1[e + q] = total
            h = total * slope0_ref[e + q + 2].astype(F32)
            a = e + q - 1
            if a < 0 or a >= rows:
                h = jnp.where(inside(lat_ref, a, rows, n_lat), h, 0.0)
            put_row(b0, e + q, h)

    w0.wait()
    for copy in late:
        copy.wait()
    for a in range(0, rows, STEP):
        g = conv_back(b0, a, STEP, w_ref.at[0])
        for q in range(STEP):
            total = adj1[a + q + 1] + g[q * n : (q + 1) * n]
            unfold_row(back, a + q, dot_t(total.astype(BF16), enc_ref[...]), q_n)
            grow = back[a + q, 0:cols, :] + adj_ref[a + q]
            diff = state_ref[:, a + q, :] - prior_ref[:, a + q, :]
            out_ref[:, a + q, :] = prec * diff + grow.T[0:v, :]


BLOCK = 1024


def observe_body(
    table_ref, cols_ref, got_ref, win_ref, wout_ref, prec_ref,
    adj_ref, first_ref, last_ref, head_ref, tail_ref, pred_ref,
    xs, slope, grid, hot, weights, fa, meta,
):
    rows, cols, _ = cols_ref.shape
    cells = rows * cols
    half = cells // 2
    tiles, per, nch = pred_ref.shape
    obs_n = tiles * per
    group = LANES // per
    prec2 = prec_ref[...] * prec_ref[...]
    c0 = cols_ref[...].reshape(cells, LANES)
    c1 = pltpu.roll(c0.astype(F32), cells - 1, 0).astype(BF16)
    xs[0] = c0
    xs[1] = c1
    xs[2] = jnp.concatenate([c0[cols:], c0[:cols]], axis=0)
    xs[3] = jnp.concatenate([c1[cols:], c1[:cols]], axis=0)
    rest = jnp.zeros((1, LANES), F32)
    for m in range(obs_n // LANES):
        total = got_ref[m * group, per : per + META, :].astype(F32)
        for g in range(1, group):
            total += got_ref[m * group + g, per : per + META, :].astype(F32)
        meta[m] = total
        rest += jnp.where(total[2:3] == table_ref[0, 4].astype(F32), 0.0, 1.0)
    trips = jnp.where(jnp.sum(rest) > 0.0, table_ref.shape[0], 1)

    def arrangement(cls, carry):
        place = [table_ref[cls, f] for f in range(4)]
        code = table_ref[cls, 4].astype(F32)

        def forward(k, c):
            at = pl.ds(k * BLOCK, BLOCK)
            x = jnp.concatenate([xs[place[f], at, :] for f in range(4)], axis=1)
            inner = dot(x, win_ref[...])
            s = sigma(inner)
            act = inner * s
            slope[at, :] = (s + act * (1.0 - s)).astype(BF16)
            grid[at, :] = dot(act.astype(BF16), wout_ref[...]).astype(BF16)
            return c

        lax.fori_loop(0, cells // BLOCK, forward, 0)
        both = jnp.concatenate([grid[0:half, :], grid[half:, :]], axis=1)
        lane = lax.broadcasted_iota(jnp.int32, (LANES, LANES), 1).astype(F32)
        sub = lax.broadcasted_iota(jnp.int32, (LANES, LANES), 0).astype(F32)
        top = float(rows // 2)
        one16, zero16 = jnp.ones((LANES, LANES), BF16), jnp.zeros((LANES, LANES), BF16)

        def gather(m, c):
            mine = meta[m, 2:3, :] == code
            row = jnp.broadcast_to(jnp.where(mine, meta[m, 0:1, :], float(rows)), (LANES, LANES))
            col = jnp.broadcast_to(meta[m, 1:2, :], (LANES, LANES))
            row_t, col_t = row.T, col.T
            local = jnp.where(row_t < top, row_t, row_t - top)
            value = jnp.where(col_t == lane, local, -1.0).astype(BF16)
            sel = jnp.concatenate(
                [jnp.where(value == jnp.asarray(t, BF16), one16, zero16) for t in range(rows // 2)],
                axis=1,
            )
            out = dot(sel, both)
            upper = row_t >= top
            pred = jnp.where(upper, out[:, nch:], out[:, :nch])
            pred = jnp.where(row_t < float(rows), pred, 0.0)
            obs = got_ref[pl.ds(m * group, group), 0:per, :].astype(F32).reshape(LANES, nch)
            w = (pred - obs) * prec2
            at = pl.ds(m * LANES, LANES)
            weights[at, 0:nch] = jnp.where(upper, 0.0, w).astype(BF16)
            weights[at, nch:] = jnp.where(upper, w, 0.0).astype(BF16)
            pred = pred.reshape(group, per, nch)
            where = pl.ds(m * group, group)

            before = jnp.where(cls > 0, pred_ref[where].astype(F32), 0.0)
            pred_ref[where] = (before + pred).astype(BF16)
            local = jnp.where(row < top, row, row - top)
            value = jnp.where(col == sub, local, -1.0).astype(BF16)
            for t in range(rows // 2):
                hot[t * LANES : (t + 1) * LANES, pl.ds(pl.multiple_of(m * LANES, LANES), LANES)] = (
                    jnp.where(value == jnp.asarray(t, BF16), one16, zero16)
                )
            return c

        lax.fori_loop(0, obs_n // LANES, gather, 0, unroll=4)

        def scatter(k, c):
            at = pl.ds(k * BLOCK, BLOCK)
            total = dot(hot[at, :], weights[...])
            grid[at, :] = total[:, :nch].astype(BF16)
            grid[pl.ds(half + k * BLOCK, BLOCK), :] = total[:, nch:].astype(BF16)
            return c

        lax.fori_loop(0, half // BLOCK, scatter, 0)

        def backward(k, c):
            at = pl.ds(k * BLOCK, BLOCK)
            act = dot_t(grid[at, :], wout_ref[...])
            inner = (act * slope[at, :].astype(F32)).astype(BF16)
            x = dot_t(inner, win_ref[...])
            for f in range(4):
                before = jnp.where(cls > 0, fa[place[f], at, :], 0.0)
                fa[place[f], at, :] = before + x[:, f * LANES : (f + 1) * LANES]
            return c

        lax.fori_loop(0, cells // BLOCK, backward, 0)
        return carry

    lax.fori_loop(0, trips, arrangement, 0)
    high = fa[3]
    one = fa[1] + jnp.concatenate([high[cells - cols :], high[: cells - cols]], axis=0)
    low = fa[2]
    total = fa[0] + jnp.concatenate([low[cells - cols :], low[: cells - cols]], axis=0)
    total += pltpu.roll(one, 1, 0)
    total = total.reshape(rows, cols, LANES)
    adj_ref[...] = total
    total = total.astype(BF16)
    for r in range(rows):
        edges(total[r], r, rows, BACK, first_ref, last_ref, head_ref, tail_ref)


def arrangement_table():
    orders = list(itertools.permutations(range(4)))
    first = (0, 2, 1, 3)
    orders.remove(first)
    return [
        list(o) + [sum(q * 4**f for f, q in enumerate(o))] for o in [first] + orders
    ]


def on_device(
    analysis_vector,
    prior_estimate,
    prior_precision,
    encoder_weight,
    conv_weights,
    readout_matrix,
    obs_in_weight,
    obs_out_weight,
    obs_values,
    obs_precision,
    foot_cells,
    obs_count,
):
    v, rows, cols = analysis_vector.shape
    n_lat, n_lon = lax.axis_size("lat"), lax.axis_size("lon")
    tiles = n_lat * n_lon
    obs_n, foot = foot_cells.shape
    per = obs_n // tiles
    ch = encoder_weight.shape[1]
    hid, nch = obs_out_weight.shape
    width = cols + 2 * EDGE
    cells = rows * cols
    lat, lon = lax.axis_index("lat"), lax.axis_index("lon")
    lat_id = lat.reshape(1)

    strip = (rows, EDGE, LANES)
    at, *rim = call(
        state_body,
        [((rows, cols, LANES), F32)]
        + [(strip, BF16)] * 2 + [((HALO, cols, LANES), BF16)] * 2,
        1, moved=cells * v * 8,
    )(analysis_vector)
    foot_cells, obs_sent, *rim = lax.optimization_barrier((foot_cells, obs_values, *rim))
    top, bottom, near, far = halo_rows(*rim)

    lon_total = cols * n_lon
    lat_g, lon_g = foot_cells // lon_total, foot_cells % lon_total
    order = lat_g[:tiles, 0] // rows * n_lon + lon_g[:tiles, 0] // cols
    base_lat, base_lon = jnp.min(lat_g, axis=1), jnp.min(lon_g, axis=1)
    place = (lat_g - base_lat[:, None]) * 2 + (lon_g - base_lon[:, None])
    code = jnp.sum(place * (4 ** jnp.arange(foot)), axis=1)
    valid = jnp.arange(obs_n) < obs_count[0]
    local = jnp.where(valid, base_lat % rows, rows)
    fields = jnp.stack([local, base_lon % cols, code]).astype(BF16).reshape(3, per, tiles)
    pick = (order[None, :] == jnp.arange(tiles)[:, None]).astype(BF16)
    meta = jnp.einsum("fkp,hp->hfk", fields, pick, preferred_element_type=F32).astype(BF16)
    group = LANES // per
    mine = jnp.arange(group) == (lat * n_lon + lon) % group
    meta = jnp.where(mine[:, None], meta[:, :, None, :], jnp.zeros((), BF16)).reshape(tiles, 3, LANES)
    meta = jnp.pad(meta, ((0, 0), (0, META - 3), (0, 0)))
    send, kept = call(
        pack_body, [((tiles, per + META, nch), BF16), ((tiles, per, nch), F32)], 3, smem=(0,), moved=obs_n * nch * 6
    )(order, obs_sent, meta)
    send, near, far = lax.optimization_barrier((send, near, far))
    right, left = halo_columns(near, far)
    got = lax.all_to_all(send, ("lat", "lon"), split_axis=0, concat_axis=0, tiled=True)

    rot = readout_matrix.T
    win = jnp.pad(obs_in_weight, ((0, 0), (0, LANES - v), (0, 0))).reshape(foot * LANES, hid)
    w_fwd = conv_weights.reshape(conv_weights.shape[0], 9 * ch, ch)

    conv_flops = 2 * cells * 9 * ch * ch
    cols16, slope0, slope1 = call(
        functools.partial(forward_body, n_lat),
        [
            ((rows, cols, LANES), BF16),
            ((rows + 2 * HALO - 2, width, ch), BF16),
            ((rows + 2 * HALO - 4, width, ch), BF16),
        ],
        9,
        [
            VMEM((rows + 2 * HALO, width // SUB + 2, SUB, ch), BF16),
            VMEM((rows + 2 * HALO - 2, width // SUB + 2, SUB, ch), BF16),
            VMEM((rows + 2 * HALO, width, LANES), F32),
            VMEM((rows, width, LANES), F32),
            VMEM((LANES, ch), BF16),
            VMEM((LANES, ch), BF16),
            VMEM(w_fwd.shape, BF16),
            VMEM((rows, cols, LANES), F32),
            VMEM((rows + 2 * HALO - 2, width, ch), BF16),
            VMEM((rows + 2 * HALO - 4, width, ch), BF16),
            pltpu.SemaphoreType.DMA((6,)),
        ],
        (0,), 3 * conv_flops, cells * ch * 8, far=(5, 7), far_out=(1, 2),
    )(lat_id, top, bottom, right, left, at, encoder_weight, w_fwd, rot)

    adj, *rim, pred = call(
        observe_body,
        [((rows, cols, LANES), F32)]
        + [(strip, BF16)] * 2 + [((BACK, cols, LANES), BF16)] * 2 + [((tiles, per, nch), BF16)],
        6,
        [
            VMEM((4, cells, LANES), BF16),
            VMEM((cells, hid), BF16),
            VMEM((cells, nch), BF16),
            VMEM((cells // 2, obs_n), BF16),
            VMEM((obs_n, 2 * nch), BF16),
            VMEM((4, cells, LANES), F32),
            VMEM((obs_n // LANES, META, LANES), F32),
        ],
        (0,), 4 * cells * hid * (foot * LANES + nch), cells * hid * 4, limit=51,
    )(
        jnp.array(arrangement_table(), jnp.int32), cols16, got, win, obs_out_weight,
        obs_precision[None, :],
    )
    back = lax.all_to_all(pred, ("lat", "lon"), split_axis=0, concat_axis=0, tiled=True)

    top, bottom, near, far = halo_rows(*rim)
    right, left = halo_columns(near, far)
    (derivative,) = call(
        functools.partial(adjoint_body, n_lat),
        [((v, rows, cols), F32)],
        14,
        [
            VMEM((rows + 2 * BACK, width // SUB + 2, SUB, ch), BF16),
            VMEM((rows + 2, width // SUB + 2, SUB, ch), BF16),
            VMEM((rows + 2 * BACK, width, ch), F32),
            VMEM((rows + 2, width, ch), F32),
            VMEM((rows + 2 * BACK, width, LANES), F32),
            VMEM((rows, width, LANES), F32),
            VMEM((LANES, ch), BF16),
            VMEM((LANES, ch), BF16),
            VMEM((8, LANES), F32),
            VMEM((rows, cols, LANES), F32),
            VMEM(slope0.shape, BF16),
            VMEM(slope1.shape, BF16),
            VMEM(w_fwd.shape, BF16),
            VMEM((v, rows, cols), F32),
            VMEM((v, rows, cols), F32),
            pltpu.SemaphoreType.DMA((7,)),
        ],
        (0,), 3 * conv_flops, cells * ch * 8, far=(5, 6, 7, 9, 11, 12),
    )(
        lat_id, top, bottom, right, left, adj, slope0, slope1, rot, w_fwd, encoder_weight,
        analysis_vector, prior_estimate, prior_precision[None, :],
    )
    departures = unpack(order, obs_count, back, kept, obs_precision[None, :])
    return departures, derivative


def solution(mesh):
    return jax.shard_map(
        on_device,
        mesh=mesh,
        in_specs=(
            P(None, "lat", "lon"),
            P(None, "lat", "lon"),
            P(),
            P(),
            P(),
            P(),
            P(),
            P(),
            P(("lat", "lon"), None),
            P(),
            P(("lat", "lon"), None),
            P(("lat", "lon")),
        ),
        out_specs=(P(("lat", "lon"), None), P(None, "lat", "lon")),
        check_vma=False,
    )
```

```python
import functools
import itertools

import jax
import jax.numpy as jnp
from jax import lax
from jax.experimental import pallas as pl
from jax.experimental.pallas import tpu as pltpu
from jax.sharding import PartitionSpec as P


F32 = jnp.float32
BF16 = jnp.bfloat16
LANES = 128
EDGE = 8
HALO = 4
BACK = 2
META = 8
CHUNK = 16
UNPACK = 50
VMEM = pltpu.VMEM
SMEM = pltpu.SMEM


def call(body, outs, n_in, scratch=(), smem=(), flops=0, moved=0, limit=53, far=(), far_out=()):
    def spec(i, far=far, smem=smem):
        space = SMEM if i in smem else pltpu.HBM if i in far else VMEM
        return pl.BlockSpec(memory_space=space)

    specs = [spec(i) for i in range(n_in)]
    return pl.pallas_call(
        body,
        out_shape=tuple(jax.ShapeDtypeStruct(s, d) for s, d in outs),
        in_specs=specs,
        out_specs=tuple(spec(i, far_out, ()) for i in range(len(outs))),
        scratch_shapes=list(scratch),
        cost_estimate=pl.CostEstimate(flops=flops, bytes_accessed=moved, transcendentals=0),
        compiler_params=pltpu.CompilerParams(vmem_limit_bytes=limit * 2**20),
    )


def sigma(v):
    return 0.5 * jnp.tanh(0.5 * v) + 0.5


def dot(a, b):
    return jnp.dot(a, b, preferred_element_type=F32)


def dot_t(a, b):
    return lax.dot_general(a, b, (((1,), (1,)), ((), ())), preferred_element_type=F32)


def fetch(src, dst, sem):
    copy = pltpu.make_async_copy(src, dst, sem)
    copy.start()
    return copy


def padded(ref, src_ref):
    ref[...] = jnp.zeros_like(ref)
    ref[0 : src_ref.shape[0], :] = src_ref[...]


def edges(half, r, rows, width, first_ref, last_ref, head_ref, tail_ref):
    first_ref[r] = half[:EDGE]
    last_ref[r] = half[half.shape[0] - EDGE :]
    if r < width:
        head_ref[r] = half
    if r >= rows - width:
        tail_ref[r - rows + width] = half


def state_body(a_ref, at_ref, first_ref, last_ref, head_ref, tail_ref):
    v, rows, cols = a_ref.shape
    pad = jnp.zeros((LANES - v, cols), F32)
    for r in range(rows):
        x = jnp.concatenate([a_ref[:, r, :], pad], axis=0).T
        at_ref[r] = x
        edges(x.astype(BF16), r, rows, HALO, first_ref, last_ref, head_ref, tail_ref)


def sides_body(top_ref, bottom_ref, first_ref, last_ref, near_ref, far_ref):
    width, cols, _ = top_ref.shape
    rows = first_ref.shape[0]
    near_ref[0:width] = top_ref[:, :EDGE]
    near_ref[width : width + rows] = first_ref[...]
    near_ref[width + rows :] = bottom_ref[:, :EDGE]
    far_ref[0:width] = top_ref[:, cols - EDGE :]
    far_ref[width : width + rows] = last_ref[...]
    far_ref[width + rows :] = bottom_ref[:, cols - EDGE :]


def pack_body(order_ref, obs_ref, meta_ref, out_ref, kept_ref):
    tiles = out_ref.shape[0]
    per = out_ref.shape[1] - META

    def one(p, c):
        h = order_ref[p]
        obs = obs_ref[pl.ds(p, per, stride=tiles), :]
        kept_ref[h] = obs
        out_ref[h, 0:per, :] = obs.astype(BF16)
        return c

    lax.fori_loop(0, tiles, one, 0, unroll=8)
    for h in range(tiles):
        out_ref[h, per : per + META, :] = meta_ref[h]


def unpack_body(order_ref, count_ref, got_ref, obs_ref, prec_ref, out_ref, out_v, sem):
    tiles, per, _ = got_ref.shape
    chunk = min(per, CHUNK)
    prec = prec_ref[...]
    slot = lax.broadcasted_iota(jnp.int32, (chunk, LANES), 0) * tiles
    sent = []
    for k in range(per // chunk):
        for p in range(tiles):
            h = order_ref[p]
            ks = slice(k * chunk, (k + 1) * chunk)
            dep = (got_ref[h, ks, :].astype(F32) - obs_ref[h, ks, :]) * prec
            first = k * chunk * tiles + p
            out_v[pl.ds(first, chunk, stride=tiles), :] = jnp.where(
                slot + first < count_ref[0], dep, 0.0
            )
        done = slice(k * chunk * tiles, (k + 1) * chunk * tiles)
        sent.append(fetch(out_v.at[done], out_ref.at[done], sem.at[k]))
    for copy in sent:
        copy.wait()


def shift_pairs(size, wrap):
    up = [(i, (i + 1) % size) for i in range(size if wrap else size - 1)]
    return up, [(j, i) for i, j in up]


def halo_rows(first, last, head, tail):
    up, down = shift_pairs(lax.axis_size("lat"), False)
    top = lax.ppermute(tail, "lat", up)
    bottom = lax.ppermute(head, "lat", down)
    shape = (first.shape[0] + 2 * head.shape[0],) + first.shape[1:]
    near, far = call(sides_body, [(shape, BF16)] * 2, 4)(
        top, bottom, first, last
    )
    return top, bottom, near, far


def halo_columns(near, far):
    up, down = shift_pairs(lax.axis_size("lon"), True)
    left = lax.ppermute(far, "lon", up)
    right = lax.ppermute(near, "lon", down)
    return right, left


def bands(mid_ref, top_ref, bottom_ref, width):
    rows = mid_ref.shape[0]
    return (
        [(top_ref, r) for r in range(width)]
        + [(mid_ref, r) for r in range(rows)]
        + [(bottom_ref, r) for r in range(width)]
    )


def fold_row(nat_ref, e, q_n):
    slabs = [nat_ref[e, pl.ds(q, SUB, stride=q_n), :] for q in range(q_n)]
    return jnp.concatenate(slabs, axis=0)


def unfold_row(nat_ref, e, value, q_n):
    for q in range(q_n):
        nat_ref[e, pl.ds(q, SUB, stride=q_n), :] = value[q * SUB : (q + 1) * SUB]


def put_row(ref, e, value):
    n, ch = value.shape
    q_n = n // SUB
    ref[e, 1 : q_n + 1] = value.astype(BF16).reshape(q_n, SUB, ch)
    ref[e, 0] = pltpu.roll(value[n - SUB :], 1, 0).astype(BF16)
    ref[e, q_n + 1] = pltpu.roll(value[:SUB], SUB - 1, 0).astype(BF16)


def center(ref, e):
    q_n, ch = ref.shape[1] - 2, ref.shape[3]
    return ref[e, 1 : q_n + 1].reshape(q_n * SUB, ch)


def conv_rows(ref, e, count, weight):
    q_n, ch = ref.shape[1] - 2, ref.shape[3]
    parts = [
        ref[e + i : e + i + count, j : j + q_n].reshape(count * q_n * SUB, ch)
        for i in range(3)
        for j in range(3)
    ]
    return dot(jnp.concatenate(parts, axis=1), weight)


def conv_back(ref, e, count, weight_ref):
    q_n, ch = ref.shape[1] - 2, ref.shape[3]
    parts = [
        ref[e + i : e + i + count, j : j + q_n].reshape(count * q_n * SUB, ch)
        for i in range(3)
        for j in range(3)
    ]
    taps = [weight_ref[(8 - t) * ch : (9 - t) * ch, :] for t in range(9)]
    return dot_t(jnp.concatenate(parts, axis=1), jnp.concatenate(taps, axis=1))


def inside(lat_ref, a, rows, n_lat):
    g = lat_ref[0] * rows + a
    return jnp.logical_and(g >= 0, g < n_lat * rows)


STEP = 2
SUB = 16


def forward_body(
    n_lat, lat_ref, top_ref, bottom_ref, right_ref, left_ref, at_ref, enc_in, w_ref, ro_in,
    cols_ref, slope0_out, slope1_out,
    a0, a1, nat, back, enc_ref, ro_ref, w_v, at_v, slope0_ref, slope1_ref, sem,
):
    at_in = fetch(at_ref, at_v, sem.at[2])
    w0 = fetch(w_ref.at[0], w_v.at[0], sem.at[0])
    w1 = fetch(w_ref.at[1], w_v.at[1], sem.at[1])
    padded(enc_ref, enc_in)
    padded(ro_ref, ro_in)
    rows, cols, _ = at_v.shape
    at_in.wait()
    q_n = a0.shape[1] - 2
    n = q_n * SUB
    for e, (src, r) in enumerate(bands(at_v, top_ref, bottom_ref, HALO)):
        nat[e, 0:cols, :] = src[r].astype(F32)
        nat[e, cols : cols + EDGE, :] = right_ref[e].astype(F32)
        nat[e, cols + EDGE :, :] = left_ref[e].astype(F32)
        x = fold_row(nat, e, q_n).astype(BF16)
        put_row(a0, e, dot(x, enc_ref[...]))

    def first(e):
        pre = conv_rows(a0, e, STEP, w_v[0])
        s = sigma(pre)
        act = pre * s
        slope = (s + act * (1.0 - s)).astype(BF16)
        for q in range(STEP):
            at = slice(q * n, (q + 1) * n)
            slope0_ref[e + q] = slope[at]
            h = center(a0, e + q + 1).astype(F32) + act[at]
            a = e + q - HALO + 1
            if a < 0 or a >= rows:
                h = jnp.where(inside(lat_ref, a, rows, n_lat), h, 0.0)
            put_row(a1, e + q, h)

    def second(e):
        pre = conv_rows(a1, e, STEP, w_v[1])
        s = sigma(pre)
        act = pre * s
        slope = (s + act * (1.0 - s)).astype(BF16)
        for q in range(STEP):
            at = slice(q * n, (q + 1) * n)
            slope1_ref[e + q] = slope[at]
            a = e + q - HALO + 2
            if 0 <= a < rows:
                h = center(a1, e + q + 1).astype(F32) + act[at]
                unfold_row(back, a, dot_t(h.astype(BF16), ro_ref[...]), q_n)
                cols_ref[a] = (at_v[a] + back[a, 0:cols, :]).astype(BF16)

    w0.wait()
    for e in range(0, rows + 2 * HALO - 2, STEP):
        first(e)
    out0 = fetch(slope0_ref, slope0_out, sem.at[3])
    w1.wait()
    half = (rows + 2 * HALO - 4) // 2
    for e in range(0, half, STEP):
        second(e)
    out1 = fetch(slope1_ref.at[0:half], slope1_out.at[0:half], sem.at[4])
    for e in range(half, 2 * half, STEP):
        second(e)
    out2 = fetch(slope1_ref.at[half:], slope1_out.at[half:], sem.at[5])
    out0.wait()
    out1.wait()
    out2.wait()


def adjoint_body(
    n_lat, lat_ref, top_ref, bottom_ref, right_ref, left_ref, adj_in, slope0_in, slope1_in,
    rot_in, w_in, enc_in, state_in, prior_in, prec_in,
    out_ref, b1, b0, adj2, adj1, nat, back, rot_ref, enc_ref, prec_pad,
    adj_ref, slope0_ref, slope1_ref, w_ref, state_ref, prior_ref, sem,
):
    adj_got = fetch(adj_in, adj_ref, sem.at[4])
    slope1_got = fetch(slope1_in, slope1_ref, sem.at[0])
    w1 = fetch(w_in.at[1], w_ref.at[1], sem.at[1])
    slope0_got = fetch(slope0_in, slope0_ref, sem.at[2])
    w0 = fetch(w_in.at[0], w_ref.at[0], sem.at[3])
    late = [
        fetch(state_in, state_ref, sem.at[5]),
        fetch(prior_in, prior_ref, sem.at[6]),
    ]
    padded(rot_ref, rot_in)
    padded(enc_ref, enc_in)
    prec_pad[...] = jnp.zeros_like(prec_pad)
    prec_pad[0:1, 0 : prec_in.shape[1]] = prec_in[...]
    rows, cols, _ = adj_ref.shape
    q_n = b1.shape[1] - 2
    n = q_n * SUB
    v = out_ref.shape[0]
    prec = jnp.broadcast_to(prec_pad[0:1, :], (LANES, LANES)).T[0:v, :]
    adj_got.wait()
    slope1_got.wait()
    for e, (src, r) in enumerate(bands(adj_ref, top_ref, bottom_ref, BACK)):
        nat[e, 0:cols, :] = src[r].astype(F32)
        nat[e, cols : cols + EDGE, :] = right_ref[e].astype(F32)
        nat[e, cols + EDGE :, :] = left_ref[e].astype(F32)
        g = dot(fold_row(nat, e, q_n).astype(BF16), rot_ref[...])
        adj2[e] = g
        put_row(b1, e, g * slope1_ref[e].astype(F32))

    slope0_got.wait()
    w1.wait()
    for e in range(0, rows + 2, STEP):
        g = conv_back(b1, e, STEP, w_ref.at[1])
        for q in range(STEP):
            total = adj2[e + q + 1] + g[q * n : (q + 1) * n]
            adj1[e + q] = total
            h = total * slope0_ref[e + q + 2].astype(F32)
            a = e + q - 1
            if a < 0 or a >= rows:
                h = jnp.where(inside(lat_ref, a, rows, n_lat), h, 0.0)
            put_row(b0, e + q, h)

    w0.wait()
    for copy in late:
        copy.wait()
    for a in range(0, rows, STEP):
        g = conv_back(b0, a, STEP, w_ref.at[0])
        for q in range(STEP):
            total = adj1[a + q + 1] + g[q * n : (q + 1) * n]
            unfold_row(back, a + q, dot_t(total.astype(BF16), enc_ref[...]), q_n)
            grow = back[a + q, 0:cols, :] + adj_ref[a + q]
            diff = state_ref[:, a + q, :] - prior_ref[:, a + q, :]
            out_ref[:, a + q, :] = prec * diff + grow.T[0:v, :]


BLOCK = 1024
BATCH = 8


def observe_body(
    table_ref, cols_ref, got_ref, win_ref, wout_ref, prec_ref,
    adj_ref, first_ref, last_ref, head_ref, tail_ref, pred_ref,
    xs, slope, grid, hot, weights, fa, meta,
):
    rows, cols, _ = cols_ref.shape
    cells = rows * cols
    half = cells // 2
    tiles, per, nch = pred_ref.shape
    obs_n = tiles * per
    group = LANES // per
    prec2 = prec_ref[...] * prec_ref[...]
    c0 = cols_ref[...].reshape(cells, LANES)
    c1 = pltpu.roll(c0.astype(F32), cells - 1, 0).astype(BF16)
    xs[0] = c0
    xs[1] = c1
    xs[2] = jnp.concatenate([c0[cols:], c0[:cols]], axis=0)
    xs[3] = jnp.concatenate([c1[cols:], c1[:cols]], axis=0)
    rest = jnp.zeros((1, LANES), F32)
    for m in range(obs_n // LANES):
        total = got_ref[m * group, per : per + META, :].astype(F32)
        for g in range(1, group):
            total += got_ref[m * group + g, per : per + META, :].astype(F32)
        meta[m] = total
        rest += jnp.where(total[2:3] == table_ref[0, 4].astype(F32), 0.0, 1.0)
    trips = jnp.where(jnp.sum(rest) > 0.0, table_ref.shape[0], 1)

    def arrangement(cls, carry):
        place = [table_ref[cls, f] for f in range(4)]
        code = table_ref[cls, 4].astype(F32)

        def forward(k, c):
            at = pl.ds(k * BLOCK, BLOCK)
            x = jnp.concatenate([xs[place[f], at, :] for f in range(4)], axis=1)
            inner = dot(x, win_ref[...])
            s = sigma(inner)
            act = inner * s
            slope[at, :] = (s + act * (1.0 - s)).astype(BF16)
            grid[at, :] = dot(act.astype(BF16), wout_ref[...]).astype(BF16)
            return c

        lax.fori_loop(0, cells // BLOCK, forward, 0)
        both = jnp.concatenate([grid[0:half, :], grid[half:, :]], axis=1)
        lane = lax.broadcasted_iota(jnp.int32, (LANES, LANES), 1).astype(F32)
        sub = lax.broadcasted_iota(jnp.int32, (LANES, LANES), 0).astype(F32)
        top = float(rows // 2)
        one16, zero16 = jnp.ones((LANES, LANES), BF16), jnp.zeros((LANES, LANES), BF16)

        def select(m):
            mine = meta[m, 2:3, :] == code
            row = jnp.broadcast_to(jnp.where(mine, meta[m, 0:1, :], float(rows)), (LANES, LANES))
            col = jnp.broadcast_to(meta[m, 1:2, :], (LANES, LANES))
            row_t, col_t = row.T, col.T
            local = jnp.where(row_t < top, row_t, row_t - top)
            value = jnp.where(col_t == lane, local, -1.0).astype(BF16)
            picks = [
                jnp.where(value == jnp.asarray(t, BF16), one16, zero16) for t in range(rows // 2)
            ]
            local = jnp.where(row < top, row, row - top)
            value = jnp.where(col == sub, local, -1.0).astype(BF16)
            for t in range(rows // 2):
                hot[t * LANES : (t + 1) * LANES, pl.ds(pl.multiple_of(m * LANES, LANES), LANES)] = (
                    jnp.where(value == jnp.asarray(t, BF16), one16, zero16)
                )
            return row_t, jnp.concatenate(picks, axis=1)

        def deposit(m, row_t, out):
            upper = row_t >= top
            pred = jnp.where(upper, out[:, nch:], out[:, :nch])
            pred = jnp.where(row_t < float(rows), pred, 0.0)
            obs = got_ref[pl.ds(m * group, group), 0:per, :].astype(F32).reshape(LANES, nch)
            w = (pred - obs) * prec2
            at = pl.ds(m * LANES, LANES)
            weights[at, 0:nch] = jnp.where(upper, 0.0, w).astype(BF16)
            weights[at, nch:] = jnp.where(upper, w, 0.0).astype(BF16)
            pred = pred.reshape(group, per, nch)
            where = pl.ds(m * group, group)
            before = jnp.where(cls > 0, pred_ref[where].astype(F32), 0.0)
            pred_ref[where] = (before + pred).astype(BF16)

        def gather(b, c):
            found = [select(b * BATCH + i) for i in range(BATCH)]
            out = dot(jnp.concatenate([picks for _, picks in found], axis=0), both)
            for i, (row_t, _) in enumerate(found):
                deposit(b * BATCH + i, row_t, out[i * LANES : (i + 1) * LANES])
            return c

        lax.fori_loop(0, obs_n // LANES // BATCH, gather, 0)

        def scatter(k, c):
            at = pl.ds(k * BLOCK, BLOCK)
            total = dot(hot[at, :], weights[...])
            grid[at, :] = total[:, :nch].astype(BF16)
            grid[pl.ds(half + k * BLOCK, BLOCK), :] = total[:, nch:].astype(BF16)
            return c

        lax.fori_loop(0, half // BLOCK, scatter, 0)

        def backward(k, c):
            at = pl.ds(k * BLOCK, BLOCK)
            act = dot_t(grid[at, :], wout_ref[...])
            inner = (act * slope[at, :].astype(F32)).astype(BF16)
            x = dot_t(inner, win_ref[...])
            for f in range(4):
                before = jnp.where(cls > 0, fa[place[f], at, :], 0.0)
                fa[place[f], at, :] = before + x[:, f * LANES : (f + 1) * LANES]
            return c

        lax.fori_loop(0, cells // BLOCK, backward, 0)
        return carry

    lax.fori_loop(0, trips, arrangement, 0)
    high = fa[3]
    one = fa[1] + jnp.concatenate([high[cells - cols :], high[: cells - cols]], axis=0)
    low = fa[2]
    total = fa[0] + jnp.concatenate([low[cells - cols :], low[: cells - cols]], axis=0)
    total += pltpu.roll(one, 1, 0)
    total = total.reshape(rows, cols, LANES)
    adj_ref[...] = total
    total = total.astype(BF16)
    for r in range(rows):
        edges(total[r], r, rows, BACK, first_ref, last_ref, head_ref, tail_ref)


def arrangement_table():
    orders = list(itertools.permutations(range(4)))
    first = (0, 2, 1, 3)
    orders.remove(first)
    return [
        list(o) + [sum(q * 4**f for f, q in enumerate(o))] for o in [first] + orders
    ]


def on_device(
    analysis_vector,
    prior_estimate,
    prior_precision,
    encoder_weight,
    conv_weights,
    readout_matrix,
    obs_in_weight,
    obs_out_weight,
    obs_values,
    obs_precision,
    foot_cells,
    obs_count,
):
    v, rows, cols = analysis_vector.shape
    n_lat, n_lon = lax.axis_size("lat"), lax.axis_size("lon")
    tiles = n_lat * n_lon
    obs_n, foot = foot_cells.shape
    per = obs_n // tiles
    ch = encoder_weight.shape[1]
    hid, nch = obs_out_weight.shape
    width = cols + 2 * EDGE
    cells = rows * cols
    lat, lon = lax.axis_index("lat"), lax.axis_index("lon")
    lat_id = lat.reshape(1)

    strip = (rows, EDGE, LANES)
    at, *rim = call(
        state_body,
        [((rows, cols, LANES), F32)]
        + [(strip, BF16)] * 2 + [((HALO, cols, LANES), BF16)] * 2,
        1, moved=cells * v * 8,
    )(analysis_vector)
    foot_cells, obs_sent, *rim = lax.optimization_barrier((foot_cells, obs_values, *rim))
    top, bottom, near, far = halo_rows(*rim)

    lon_total = cols * n_lon
    lat_g, lon_g = foot_cells // lon_total, foot_cells % lon_total
    order = lat_g[:tiles, 0] // rows * n_lon + lon_g[:tiles, 0] // cols
    base_lat, base_lon = jnp.min(lat_g, axis=1), jnp.min(lon_g, axis=1)
    place = (lat_g - base_lat[:, None]) * 2 + (lon_g - base_lon[:, None])
    code = jnp.sum(place * (4 ** jnp.arange(foot)), axis=1)
    valid = jnp.arange(obs_n) < obs_count[0]
    local = jnp.where(valid, base_lat % rows, rows)
    fields = jnp.stack([local, base_lon % cols, code]).astype(BF16).reshape(3, per, tiles)
    pick = (order[None, :] == jnp.arange(tiles)[:, None]).astype(BF16)
    meta = jnp.einsum("fkp,hp->hfk", fields, pick, preferred_element_type=F32).astype(BF16)
    group = LANES // per
    mine = jnp.arange(group) == (lat * n_lon + lon) % group
    meta = jnp.where(mine[:, None], meta[:, :, None, :], jnp.zeros((), BF16)).reshape(tiles, 3, LANES)
    meta = jnp.pad(meta, ((0, 0), (0, META - 3), (0, 0)))
    send, kept = call(
        pack_body, [((tiles, per + META, nch), BF16), ((tiles, per, nch), F32)], 3, smem=(0,), moved=obs_n * nch * 6
    )(order, obs_sent, meta)
    send, near, far = lax.optimization_barrier((send, near, far))
    right, left = halo_columns(near, far)
    got = lax.all_to_all(send, ("lat", "lon"), split_axis=0, concat_axis=0, tiled=True)

    rot = readout_matrix.T
    win = jnp.pad(obs_in_weight, ((0, 0), (0, LANES - v), (0, 0))).reshape(foot * LANES, hid)
    w_fwd = conv_weights.reshape(conv_weights.shape[0], 9 * ch, ch)

    conv_flops = 2 * cells * 9 * ch * ch
    cols16, slope0, slope1 = call(
        functools.partial(forward_body, n_lat),
        [
            ((rows, cols, LANES), BF16),
            ((rows + 2 * HALO - 2, width, ch), BF16),
            ((rows + 2 * HALO - 4, width, ch), BF16),
        ],
        9,
        [
            VMEM((rows + 2 * HALO, width // SUB + 2, SUB, ch), BF16),
            VMEM((rows + 2 * HALO - 2, width // SUB + 2, SUB, ch), BF16),
            VMEM((rows + 2 * HALO, width, LANES), F32),
            VMEM((rows, width, LANES), F32),
            VMEM((LANES, ch), BF16),
            VMEM((LANES, ch), BF16),
            VMEM(w_fwd.shape, BF16),
            VMEM((rows, cols, LANES), F32),
            VMEM((rows + 2 * HALO - 2, width, ch), BF16),
            VMEM((rows + 2 * HALO - 4, width, ch), BF16),
            pltpu.SemaphoreType.DMA((6,)),
        ],
        (0,), 3 * conv_flops, cells * ch * 8, far=(5, 7), far_out=(1, 2),
    )(lat_id, top, bottom, right, left, at, encoder_weight, w_fwd, rot)

    adj, *rim, pred = call(
        observe_body,
        [((rows, cols, LANES), F32)]
        + [(strip, BF16)] * 2 + [((BACK, cols, LANES), BF16)] * 2 + [((tiles, per, nch), BF16)],
        6,
        [
            VMEM((4, cells, LANES), BF16),
            VMEM((cells, hid), BF16),
            VMEM((cells, nch), BF16),
            VMEM((cells // 2, obs_n), BF16),
            VMEM((obs_n, 2 * nch), BF16),
            VMEM((4, cells, LANES), F32),
            VMEM((obs_n // LANES, META, LANES), F32),
        ],
        (0,), 4 * cells * hid * (foot * LANES + nch), cells * hid * 4, limit=51,
    )(
        jnp.array(arrangement_table(), jnp.int32), cols16, got, win, obs_out_weight,
        obs_precision[None, :],
    )
    back = lax.all_to_all(pred, ("lat", "lon"), split_axis=0, concat_axis=0, tiled=True)

    top, bottom, near, far = halo_rows(*rim)
    right, left = halo_columns(near, far)
    (derivative,) = call(
        functools.partial(adjoint_body, n_lat),
        [((v, rows, cols), F32)],
        14,
        [
            VMEM((rows + 2 * BACK, width // SUB + 2, SUB, ch), BF16),
            VMEM((rows + 2, width // SUB + 2, SUB, ch), BF16),
            VMEM((rows + 2 * BACK, width, ch), F32),
            VMEM((rows + 2, width, ch), F32),
            VMEM((rows + 2 * BACK, width, LANES), F32),
            VMEM((rows, width, LANES), F32),
            VMEM((LANES, ch), BF16),
            VMEM((LANES, ch), BF16),
            VMEM((8, LANES), F32),
            VMEM((rows, cols, LANES), F32),
            VMEM(slope0.shape, BF16),
            VMEM(slope1.shape, BF16),
            VMEM(w_fwd.shape, BF16),
            VMEM((v, rows, cols), F32),
            VMEM((v, rows, cols), F32),
            pltpu.SemaphoreType.DMA((7,)),
        ],
        (0,), 3 * conv_flops, cells * ch * 8, far=(5, 6, 7, 9, 11, 12),
    )(
        lat_id, top, bottom, right, left, adj, slope0, slope1, rot, w_fwd, encoder_weight,
        analysis_vector, prior_estimate, prior_precision[None, :],
    )
    (departures,) = call(
        unpack_body, [((obs_n, nch), F32)], 5,
        [VMEM((obs_n, nch), F32), pltpu.SemaphoreType.DMA((per // min(per, CHUNK),))],
        (0, 1), moved=obs_n * nch * 10, limit=UNPACK, far_out=(0,),
    )(order, obs_count, back, kept, obs_precision[None, :])
    return departures, derivative


def solution(mesh):
    return jax.shard_map(
        on_device,
        mesh=mesh,
        in_specs=(
            P(None, "lat", "lon"),
            P(None, "lat", "lon"),
            P(),
            P(),
            P(),
            P(),
            P(),
            P(),
            P(("lat", "lon"), None),
            P(),
            P(("lat", "lon"), None),
            P(("lat", "lon")),
        ),
        out_specs=(P(("lat", "lon"), None), P(None, "lat", "lon")),
        check_vma=False,
    )
```
